32 devices in a mesh: dp: 8 (over y, x, core), tensor: 4 (over z).
Axes of the slice: x: 2, y: 2, z: 4, core: 2. Of those that a mesh axis runs over, the one named last changes fastest.
Arguments:
- gate_pre: bfloat16 [2, 768, 5120], P(None, 'dp', 'tensor'), may hold values from -6 to 6
- up_pre: bfloat16 [2, 768, 5120], P(None, 'dp', 'tensor'), may hold values from -6 to 6
- down_blocks: bfloat16 [4, 32, 128, 128], P('tensor'), may hold values from -0.25 to 0.25
- block_index: int32 [4, 32], P('tensor'), may hold values from 0 to 319, as said below
- out_grad: bfloat16 [2, 768, 4096], P(None, ('dp', 'tensor')), may hold values from -6 to 6
Outputs:
- layer_out: bfloat16 [2, 768, 4096], P(None, ('dp', 'tensor'))
- gate_grad: bfloat16 [2, 768, 5120], P(None, 'dp', 'tensor')
- up_grad: bfloat16 [2, 768, 5120], P(None, 'dp', 'tensor')
- block_grad: float32 [4, 4096, 128], P('tensor', 'dp')
The draws below stay inside these ranges and needn't reach their ends.
Inputs may be any that keep to these rules, and one draw needn't show every extreme that they name: Each row of block_index lists 32 distinct positions; position p stands for hidden block p // 32 of that tensor index and output block p % 32. Every row holds position 0 and position 319.
All inputs are finite; a program needn't handle non-finite values.
Results may differ from the reference program's by a relative error of at most 0.008.
Values may be sent and summed in bfloat16 or wider, within the bound.
No kernel may reach another device: no remote copies, remote signals or barrier semaphores. Data moves between devices by JAX's collectives and lax.ppermute only.
A program may use at most 64 MiB of HBM per device.

```python
import jax
import jax.numpy as jnp
from jax import lax

BLK = 128
D = 4096
HB_DEV = 10
NNZ_DEV = 32
MICRO = 2
DB = 32
SHARDS = 4
REPLICAS = 8
FF = 5120
MB_TOKENS = 768
FAN = 512


def draw_block_index(key, part):
    span = HB_DEV * DB

    def one_list(list_key):
        middle = jax.random.permutation(list_key, span - 2).astype(jnp.int32) + 1
        ends = jnp.array([0, span - 1], dtype=jnp.int32)
        chosen = jnp.concatenate([ends, middle[:NNZ_DEV - 2]])
        return jax.random.permutation(jax.random.fold_in(list_key, 7), chosen).astype(jnp.int32)
    list_keys = jax.random.split(key, SHARDS)
    return jax.vmap(one_list)(list_keys)


def shard_levels(rng, extent, cuts, least, top_value):
    def one(dim, parts):
        heights = jax.random.uniform(jax.random.fold_in(jax.random.fold_in(rng, 6), dim), (parts,), jnp.float32, least / len(cuts), top_value / len(cuts))
        return jnp.repeat(jnp.exp(heights), extent[dim] // parts).reshape((-1,) + (1,) * (len(extent) - dim - 1))

    loudness = one(*cuts[0])
    for cut in cuts[1:]:
        loudness = loudness * one(*cut)
    return loudness


def noise(stream_key, extent, scale, bound, cuts=(), kind=jnp.bfloat16):
    drawn = jax.random.normal(stream_key, extent, jnp.float32) * scale
    if len(cuts) > 0:
        drawn = shard_levels(stream_key, extent, cuts, -0.22, 0.18) * drawn
    return jnp.clip(drawn, min=-bound, max=bound).astype(kind)


def setup_inputs(seed: int = 0) -> dict:
    key_of = jax.random.split(jax.random.key(seed), 6)
    return {
        "gate_pre": noise(key_of[0], (MICRO, MB_TOKENS, FF), 1.0, 6.0, ((1, 8), (2, 4))),
        "up_pre": noise(key_of[1], (MICRO, MB_TOKENS, FF), 1.0, 6.0, ((1, 8), (2, 4))),
        "down_blocks": noise(key_of[2], (SHARDS, NNZ_DEV, BLK, BLK), FAN ** -0.5, 0.25, ((0, 4),)),
        "block_index": draw_block_index(jax.random.fold_in(key_of[5], 71), 0),
        "out_grad": noise(key_of[4], (MICRO, MB_TOKENS, D), 1.0, 6.0, ((1, 32),)),
    }


def reference(gate_pre, up_pre, down_blocks, block_index, out_grad):
    row_total = MICRO * MB_TOKENS
    slab_width = HB_DEV * BLK
    gate_flat = gate_pre.reshape(row_total, FF)
    up_flat = up_pre.reshape(row_total, FF)
    cot_flat = out_grad.reshape(row_total, D)

    def shard_step(running, inputs):
        weights, positions, shard_number = inputs
        slab_start = (shard_number * slab_width).astype(jnp.int32)
        gate_vals = lax.dynamic_slice_in_dim(gate_flat, slab_start, slab_width, 1).astype(jnp.float32)
        up_vals = lax.dynamic_slice_in_dim(up_flat, slab_start, slab_width, 1).astype(jnp.float32)
        gate_sigmoid = jax.nn.sigmoid(gate_vals)
        gate_silu = gate_vals * gate_sigmoid
        hidden = (gate_silu * up_vals).astype(jnp.bfloat16)

        def block_step(totals, block_item):
            partial_out, hidden_grad = totals
            weight, position = block_item
            hidden_start = ((position // DB) * BLK).astype(jnp.int32)
            output_start = ((position % DB) * BLK).astype(jnp.int32)
            hidden_cols = lax.dynamic_slice_in_dim(hidden, hidden_start, BLK, 1)
            cot_cols = lax.dynamic_slice_in_dim(cot_flat, output_start, BLK, 1)
            current_out = lax.dynamic_slice_in_dim(partial_out, output_start, BLK, 1)
            product_out = jnp.dot(hidden_cols, weight, preferred_element_type=jnp.float32)
            partial_out = lax.dynamic_update_slice_in_dim(partial_out, current_out + product_out, output_start, 1)
            current_grad = lax.dynamic_slice_in_dim(hidden_grad, hidden_start, BLK, 1)
            product_grad = jnp.dot(cot_cols, weight.T, preferred_element_type=jnp.float32)
            hidden_grad = lax.dynamic_update_slice_in_dim(hidden_grad, current_grad + product_grad, hidden_start, 1)
            one_grad = jnp.dot(hidden_cols.T, cot_cols, preferred_element_type=jnp.float32)
            return (partial_out, hidden_grad), one_grad

        initial = (jnp.zeros((row_total, D), jnp.float32), jnp.zeros((row_total, slab_width), jnp.float32))
        (partial_out, hidden_grad), block_grads = lax.scan(block_step, initial, (weights, positions))
        rounded = lax.optimization_barrier(partial_out.astype(jnp.bfloat16))
        running = running + rounded.astype(jnp.float32)
        gate_part = (hidden_grad * up_vals * gate_sigmoid * (1.0 + gate_vals * (1.0 - gate_sigmoid))).astype(jnp.bfloat16)
        up_part = (hidden_grad * gate_silu).astype(jnp.bfloat16)
        return running, (gate_part, up_part, block_grads)

    shard_numbers = jnp.arange(SHARDS, dtype=jnp.int32)
    summed, (gate_parts, up_parts, grad_parts) = lax.scan(
        shard_step, jnp.zeros((row_total, D), jnp.float32), (down_blocks, block_index, shard_numbers))
    layer_out = summed.astype(jnp.bfloat16).reshape(MICRO, MB_TOKENS, D)
    gate_grad = jnp.transpose(gate_parts, (1, 0, 2)).reshape(MICRO, MB_TOKENS, FF)
    up_grad = jnp.transpose(up_parts, (1, 0, 2)).reshape(MICRO, MB_TOKENS, FF)
    block_grad = grad_parts.reshape(SHARDS, NNZ_DEV * BLK, BLK) / REPLICAS
    return layer_out, gate_grad, up_grad, block_grad
```

```python
import functools

import jax
import jax.numpy as jnp
from jax import lax
from jax.experimental import pallas as pl
from jax.experimental.pallas import tpu as pltpu
from jax.sharding import PartitionSpec as P

BLK = 128
STREAMS = 2


def lanes(block):
    return pl.ds(pl.multiple_of(block * BLK, BLK), BLK)


def forward_kernel(pos_ref, gate_ref, up_ref, w_ref, *refs, out_blocks, streams):
    p_refs = refs[:streams]
    hid_t_ref, hid_ref, prod_ref, acc_ref = refs[streams:]
    micro, shard_count, own, width = gate_ref.shape
    rows = micro * own
    for j in range(shard_count):
        parts = []
        for m in range(micro):
            g = gate_ref[m, j].astype(jnp.float32)
            u = up_ref[m, j].astype(jnp.float32)
            parts.append(g * jax.nn.sigmoid(g) * u)
        hid_ref[pl.ds(j * rows, rows), :] = jnp.concatenate(parts, axis=0).astype(jnp.bfloat16)
    list_len = w_ref.shape[0]
    for n in range(list_len):
        c = pos_ref[n] // out_blocks
        prod_ref[n] = jnp.dot(hid_ref[:, lanes(c)], w_ref[n], preferred_element_type=jnp.float32)
    acc_ref[...] = jnp.zeros_like(acc_ref)
    for n in range(list_len):
        r = pos_ref[n] % out_blocks
        acc_ref[r] += prod_ref[n]
    per = out_blocks // streams
    for r in range(out_blocks):
        block = acc_ref[r].astype(jnp.bfloat16)
        for j in range(shard_count):
            p_refs[r // per][j, :, pl.ds((r % per) * BLK, BLK)] = block[j * rows:(j + 1) * rows]
    for c in range(width // BLK):
        hid_t_ref[pl.ds(c * BLK, BLK), :] = hid_ref[:, pl.ds(c * BLK, BLK)].T


def block_grad_kernel(pos_ref, place_ref, *refs, out_blocks, streams, shard_count, replicas):
    own_refs = refs[:streams]
    count = (shard_count - 1) * streams
    right_refs = refs[streams:streams + count]
    left_refs = refs[streams + count:streams + 2 * count]
    hid_t_ref, keep_ref, send_ref, cot_ref = refs[streams + 2 * count:]
    rows, span = own_refs[0].shape
    i = place_ref[0]
    core = place_ref[1]
    for h in range(streams):
        cols = pl.ds(h * span, span)
        cot_ref[pl.ds(pl.multiple_of(i * rows, rows), rows), cols] = own_refs[h][...]
        for k in range(1, shard_count):
            right = right_refs[(k - 1) * streams + h]
            left = left_refs[(k - 1) * streams + h]

            @pl.when(k <= i)
            def _(k=k, right=right, cols=cols):
                cot_ref[pl.ds(pl.multiple_of((i - k) * rows, rows), rows), cols] = right[...]

            @pl.when(i + k < shard_count)
            def _(k=k, left=left, cols=cols):
                cot_ref[pl.ds(pl.multiple_of((i + k) * rows, rows), rows), cols] = left[...]
    list_len = pos_ref.shape[0]
    owned = list_len * BLK // replicas
    for n in range(list_len):
        c = pos_ref[n] // out_blocks
        r = pos_ref[n] % out_blocks
        grad = jnp.dot(
            hid_t_ref[lanes(c), :], cot_ref[:, lanes(r)], preferred_element_type=jnp.float32
        )
        piece = min(owned, BLK)
        for s in range(BLK // piece):
            owner, offset = divmod(n * BLK + s * piece, owned)
            value = grad[s * piece:(s + 1) * piece]

            @pl.when(owner % 2 == core)
            def _(owner=owner, offset=offset, value=value):
                keep_ref[owner // 2, pl.ds(offset, piece), :] = value

            @pl.when(owner % 2 != core)
            def _(owner=owner, offset=offset, value=value):
                send_ref[owner // 2, pl.ds(offset, piece), :] = value.astype(jnp.bfloat16)


def hidden_grad_kernel(pos_ref, cot_ref, w_ref, gate_ref, up_ref, gg_ref, ug_ref, prod_ref, acc_ref, *, out_blocks):
    micro, shard_count, own, width = gate_ref.shape
    rows = micro * own
    list_len = w_ref.shape[0]
    for n in range(list_len):
        r = pos_ref[n] % out_blocks
        prod_ref[n] = lax.dot_general(
            cot_ref[:, lanes(r)], w_ref[n], (((1,), (1,)), ((), ())), preferred_element_type=jnp.float32
        )
    acc_ref[...] = jnp.zeros_like(acc_ref)
    for n in range(list_len):
        c = pos_ref[n] // out_blocks
        acc_ref[c] += prod_ref[n]
    for c in range(width // BLK):
        cols = pl.ds(c * BLK, BLK)
        for j in range(shard_count):
            for m in range(micro):
                hg = acc_ref[c, pl.ds(j * rows + m * own, own), :]
                g = gate_ref[m, j, :, cols].astype(jnp.float32)
                u = up_ref[m, j, :, cols].astype(jnp.float32)
                s = jax.nn.sigmoid(g)
                gg_ref[m, j, :, cols] = (hg * u * s * (1.0 + g * (1.0 - s))).astype(jnp.bfloat16)
                ug_ref[m, j, :, cols] = (hg * (g * s)).astype(jnp.bfloat16)


def shards(gate_pre, up_pre, down_blocks, block_index, out_grad):
    shard_count = lax.axis_size("tensor")
    replicas = lax.axis_size("dp")
    i = lax.axis_index("tensor")
    d = lax.axis_index("dp")
    micro, token_rows, width = gate_pre.shape
    own = out_grad.shape[1]
    features = out_grad.shape[2]
    out_blocks = features // BLK
    rows = micro * own
    tokens = micro * token_rows
    list_len = block_index.shape[1]
    span = features // STREAMS
    weights = down_blocks[0]
    positions = block_index[0]
    gate = gate_pre.reshape(micro, shard_count, own, width)
    up = up_pre.reshape(micro, shard_count, own, width)
    cot_own = out_grad.reshape(rows, features)
    own_parts = [cot_own[:, h * span:(h + 1) * span] for h in range(STREAMS)]
    vmem = pl.BlockSpec(memory_space=pltpu.VMEM)
    smem = pl.BlockSpec(memory_space=pltpu.SMEM)

    *partials, hid_t = pl.pallas_call(
        functools.partial(forward_kernel, out_blocks=out_blocks, streams=STREAMS),
        out_shape=[jax.ShapeDtypeStruct((shard_count, rows, span), jnp.bfloat16)] * STREAMS
        + [jax.ShapeDtypeStruct((width, tokens), jnp.bfloat16)],
        in_specs=[smem, vmem, vmem, vmem],
        out_specs=[vmem] * (STREAMS + 1),
        scratch_shapes=[
            pltpu.VMEM((tokens, width), jnp.bfloat16),
            pltpu.VMEM((list_len, tokens, BLK), jnp.float32),
            pltpu.VMEM((out_blocks, tokens, BLK), jnp.float32),
        ],
        name="forward",
    )(positions, gate, up, weights)

    to_right = [(s, s + 1) for s in range(shard_count - 1)]
    to_left = [(s + 1, s) for s in range(shard_count - 1)]

    def with_partial(received, partial, step, place, target):
        mine = lax.dynamic_index_in_dim(partial, jnp.clip(target, 0, shard_count - 1), 0, keepdims=False)
        both = (received.astype(jnp.float32) + mine.astype(jnp.float32)).astype(jnp.bfloat16)
        return jnp.where(step >= place + 2, both, received)

    send_right = list(own_parts)
    send_left = list(own_parts)
    right_got = []
    left_got = []
    for step in range(1, shard_count + 1):
        for h in range(STREAMS):
            got_right = lax.ppermute(send_right[h], "tensor", to_right)
            got_left = lax.ppermute(send_left[h], "tensor", to_left)
            right_got.append(got_right)
            left_got.append(got_left)
            if step < shard_count:
                nxt = step + 1
                send_right[h] = with_partial(got_right, partials[h], nxt, i, shard_count + 1 + i - nxt)
                mirror = shard_count - 1 - i
                send_left[h] = with_partial(got_left, partials[h], nxt, mirror, nxt - 2 - mirror)
    layer_parts = []
    for h in range(STREAMS):
        mine = lax.dynamic_index_in_dim(partials[h], i, 0, keepdims=False).astype(jnp.float32)
        last = (shard_count - 1) * STREAMS + h
        total = mine + right_got[last].astype(jnp.float32) + left_got[last].astype(jnp.float32)
        layer_parts.append(total.astype(jnp.bfloat16))
    layer_out = jnp.concatenate(layer_parts, axis=1).reshape(micro, own, features)

    count = (shard_count - 1) * STREAMS
    owned = list_len * BLK // replicas
    half = replicas // 2
    core = d % 2
    chip = d // 2
    keep, send, cot_all = pl.pallas_call(
        functools.partial(
            block_grad_kernel, out_blocks=out_blocks, streams=STREAMS, shard_count=shard_count, replicas=replicas
        ),
        out_shape=[
            jax.ShapeDtypeStruct((half, owned, BLK), jnp.float32),
            jax.ShapeDtypeStruct((half, owned, BLK), jnp.bfloat16),
            jax.ShapeDtypeStruct((tokens, features), jnp.bfloat16),
        ],
        in_specs=[smem, smem] + [vmem] * (STREAMS + 2 * count + 1),
        out_specs=[vmem] * 3,
        name="block_grad",
    )(positions, jnp.stack([i, core]), *own_parts, *right_got[:count], *left_got[:count], hid_t)

    from_core = lax.ppermute(send, "dp", [(s, s ^ 1) for s in range(replicas)])

    def pair_sum(index):
        a = lax.dynamic_index_in_dim(keep, index, 0, keepdims=False)
        b = lax.dynamic_index_in_dim(from_core, index, 0, keepdims=False)
        return a + b.astype(jnp.float32)

    total = pair_sum(chip)
    for s in range(1, half):
        piece = pair_sum(jnp.bitwise_xor(chip, s)).astype(jnp.bfloat16)
        got = lax.ppermute(piece, "dp", [(e, e ^ (2 * s)) for e in range(replicas)])
        total = total + got.astype(jnp.float32)
    block_grad = (total / replicas)[None]

    gate_grad, up_grad = pl.pallas_call(
        functools.partial(hidden_grad_kernel, out_blocks=out_blocks),
        out_shape=[jax.ShapeDtypeStruct((micro, shard_count, own, width), jnp.bfloat16)] * 2,
        in_specs=[smem] + [vmem] * 4,
        out_specs=[vmem] * 2,
        scratch_shapes=[
            pltpu.VMEM((list_len, tokens, BLK), jnp.float32),
            pltpu.VMEM((width // BLK, tokens, BLK), jnp.float32),
        ],
        name="hidden_grad",
    )(positions, cot_all, weights, gate, up)
    return layer_out, gate_grad.reshape(gate_pre.shape), up_grad.reshape(up_pre.shape), block_grad


def solution(mesh):
    return jax.shard_map(
        shards,
        mesh=mesh,
        in_specs=(
            P(None, "dp", "tensor"),
            P(None, "dp", "tensor"),
            P("tensor", None, None, None),
            P("tensor", None),
            P(None, ("dp", "tensor"), None),
        ),
        out_specs=(
            P(None, ("dp", "tensor"), None),
            P(None, "dp", "tensor"),
            P(None, "dp", "tensor"),
            P("tensor", "dp", None),
        ),
        check_vma=False,
    )
```

```python
import functools

import jax
import jax.numpy as jnp
from jax import lax
from jax.experimental import pallas as pl
from jax.experimental.pallas import tpu as pltpu
from jax.sharding import PartitionSpec as P

BLK = 128
VMEM_LIMIT = 24 << 20


def in_vmem(value):
    return pltpu.with_memory_space_constraint(value, pltpu.VMEM)


def in_hbm(value):
    return pltpu.with_memory_space_constraint(value, pltpu.HBM)


def lanes(block):
    return pl.ds(pl.multiple_of(block * BLK, BLK), BLK)


def sources(place, shard_count, step, even):
    parity_right = (place % 2 == 0) == even if isinstance(place, int) else (place % 2 == 0) if even else (place % 2 != 0)
    if isinstance(place, int):
        return place + step if parity_right else place - step
    return jnp.where(parity_right, place + step, place - step)


def brings_rows(shard_count, step, even):
    return any(0 <= sources(s, shard_count, step, even) < shard_count for s in range(shard_count))


def forward_kernel(pos_ref, gate_ref, up_ref, w_ref, own_ref, p_ref, hid_t_ref, own_out_ref, hid_ref, prod_ref, acc_ref):
    micro, shard_count, own, width = gate_ref.shape
    out_blocks = p_ref.shape[2] // BLK
    rows = micro * own
    own_out_ref[...] = own_ref[...]
    for j in range(shard_count):
        parts = []
        for m in range(micro):
            g = gate_ref[m, j].astype(jnp.float32)
            u = up_ref[m, j].astype(jnp.float32)
            parts.append(g * jax.nn.sigmoid(g) * u)
        hid_ref[pl.ds(j * rows, rows), :] = jnp.concatenate(parts, axis=0).astype(jnp.bfloat16)
    list_len = w_ref.shape[0]
    for n in range(list_len):
        c = pos_ref[n] // out_blocks
        prod_ref[n] = jnp.dot(hid_ref[:, lanes(c)], w_ref[n], preferred_element_type=jnp.float32)
    acc_ref[...] = jnp.zeros_like(acc_ref)
    for n in range(list_len):
        r = pos_ref[n] % out_blocks
        acc_ref[r] += prod_ref[n]
    for r in range(out_blocks):
        for j in range(shard_count):
            p_ref[j, :, pl.ds(r * BLK, BLK)] = acc_ref[r, pl.ds(j * rows, rows), :].astype(jnp.bfloat16)
    for c in range(width // BLK):
        hid_t_ref[pl.ds(c * BLK, BLK), :] = hid_ref[:, pl.ds(c * BLK, BLK)].T


def relay_kernel(got_ref, p_ref, *refs, step, even):
    send_ref = refs[-1]
    shard_count = p_ref.shape[0]
    i = lax.axis_index("tensor")
    mirror = shard_count - 1 - i
    rightward = i % 2 == 0 if even else i % 2 != 0
    place = jnp.where(rightward, i, mirror)
    target = jnp.where(rightward, shard_count + 1 + i - step, step - 2 - mirror)
    adds = step >= place + 2
    first = place == 0

    @pl.when(first)
    def _():
        send_ref[...] = p_ref[target]

    @pl.when(jnp.logical_and(adds, jnp.logical_not(first)))
    def _():
        send_ref[...] = (got_ref[...].astype(jnp.float32) + p_ref[target].astype(jnp.float32)).astype(jnp.bfloat16)

    @pl.when(jnp.logical_not(adds))
    def _():
        send_ref[...] = got_ref[...]


def layer_kernel(even_got_ref, odd_got_ref, p_ref, token_ref, out_ref):
    shard_count = p_ref.shape[0]
    i = lax.axis_index("tensor")
    even_alone = jnp.logical_and(i % 2 == 0, i == shard_count - 1)
    odd_alone = jnp.logical_or(i == 0, jnp.logical_and(i % 2 != 0, i == shard_count - 1))
    mine = p_ref[i].astype(jnp.float32)

    @pl.when(jnp.logical_not(jnp.logical_or(even_alone, odd_alone)))
    def _():
        out_ref[...] = (mine + even_got_ref[...].astype(jnp.float32) + odd_got_ref[...].astype(jnp.float32)).astype(jnp.bfloat16)

    @pl.when(odd_alone)
    def _():
        out_ref[...] = (mine + even_got_ref[...].astype(jnp.float32)).astype(jnp.bfloat16)

    @pl.when(even_alone)
    def _():
        out_ref[...] = (mine + odd_got_ref[...].astype(jnp.float32)).astype(jnp.bfloat16)


def block_grad_kernel(pos_ref, own_ref, *refs, shard_count, kinds):
    gots = refs[:len(kinds)]
    hid_t_ref, grad_ref, send_ref, cot_ref, token_ref = refs[len(kinds):]
    rows, features = own_ref.shape
    out_blocks = features // BLK
    i = lax.axis_index("tensor")
    core = lax.axis_index("dp") % 2

    def rows_of(j):
        return pl.ds(pl.multiple_of(j * rows, rows), rows)

    cot_ref[rows_of(i), :] = own_ref[...]
    for got_ref, (step, even) in zip(gots, kinds):
        source = sources(i, shard_count, step, even)

        @pl.when(jnp.logical_and(source >= 0, source < shard_count))
        def _(got_ref=got_ref, source=source):
            cot_ref[rows_of(source), :] = got_ref[...]

    for n in range(pos_ref.shape[0]):
        c = pos_ref[n] // out_blocks
        r = pos_ref[n] % out_blocks
        grad_ref[pl.ds(n * BLK, BLK), :] = jnp.dot(
            hid_t_ref[lanes(c), :], cot_ref[:, lanes(r)], preferred_element_type=jnp.float32
        )
    half, owned, _ = send_ref.shape
    for q in range(half):
        first = pl.multiple_of((2 * q + 1 - core) * owned, owned)
        send_ref[q] = grad_ref[pl.ds(first, owned), :].astype(jnp.bfloat16)
    token_ref[...] = jnp.zeros_like(token_ref)


def pair_kernel(grad_ref, got_ref, *refs):
    own_ref, token_ref = refs[-2:]
    half, owned, _ = got_ref.shape
    d = lax.axis_index("dp")
    core = d % 2
    chip = d // 2

    def pair_sum(q):
        first = pl.multiple_of((2 * q + core) * owned, owned)
        return grad_ref[pl.ds(first, owned), :] + got_ref[q].astype(jnp.float32)

    for s in range(1, half):
        refs[s - 1][...] = pair_sum(jnp.bitwise_xor(chip, s)).astype(jnp.bfloat16)
    own_ref[...] = pair_sum(chip)
    token_ref[...] = jnp.zeros_like(token_ref)


def total_kernel(own_ref, *refs, replicas):
    total = own_ref[...]
    for got_ref in refs[:-1]:
        total = total + got_ref[...].astype(jnp.float32)
    refs[-1][...] = total * (1.0 / replicas)


def hidden_grad_kernel(pos_ref, cot_ref, w_ref, gate_ref, up_ref, token_ref, gg_ref, ug_ref, token_out_ref, prod_ref, acc_ref):
    micro, shard_count, own, width = gate_ref.shape
    out_blocks = cot_ref.shape[1] // BLK
    rows = micro * own
    list_len = w_ref.shape[0]
    for n in range(list_len):
        r = pos_ref[n] % out_blocks
        prod_ref[n] = lax.dot_general(
            cot_ref[:, lanes(r)], w_ref[n], (((1,), (1,)), ((), ())), preferred_element_type=jnp.float32
        )
    acc_ref[...] = jnp.zeros_like(acc_ref)
    for n in range(list_len):
        c = pos_ref[n] // out_blocks
        acc_ref[c] += prod_ref[n]
    for c in range(width // BLK):
        cols = pl.ds(c * BLK, BLK)
        for j in range(shard_count):
            for m in range(micro):
                hg = acc_ref[c, pl.ds(j * rows + m * own, own), :]
                g = gate_ref[m, j, :, cols].astype(jnp.float32)
                u = up_ref[m, j, :, cols].astype(jnp.float32)
                s = jax.nn.sigmoid(g)
                gg_ref[m, j, :, cols] = (hg * u * s * (1.0 + g * (1.0 - s))).astype(jnp.bfloat16)
                ug_ref[m, j, :, cols] = (hg * (g * s)).astype(jnp.bfloat16)
    token_out_ref[...] = jnp.zeros_like(token_out_ref)


def neighbour_pairs(size, first):
    table = list(range(size))
    for s in range(first, size - 1, 2):
        table[s], table[s + 1] = s + 1, s
    return [(s, table[s]) for s in range(size)]


def shards(gate_pre, up_pre, down_blocks, block_index, out_grad):
    shard_count = lax.axis_size("tensor")
    replicas = lax.axis_size("dp")
    micro, token_rows, width = gate_pre.shape
    own = out_grad.shape[1]
    features = out_grad.shape[2]
    out_blocks = features // BLK
    rows = micro * own
    tokens = micro * token_rows
    list_len = block_index.shape[1]
    owned = list_len * BLK // replicas
    half = replicas // 2
    weights = in_hbm(down_blocks[0])
    gate = in_hbm(gate_pre.reshape(micro, shard_count, own, width))
    up = in_hbm(up_pre.reshape(micro, shard_count, own, width))
    cot_own = out_grad.reshape(rows, features)
    positions = block_index[0]
    vmem = pl.BlockSpec(memory_space=pltpu.VMEM)
    smem = pl.BlockSpec(memory_space=pltpu.SMEM)

    def call(kernel, name, ins, outs, scratch=(), **static):
        spec = {True: smem, False: vmem}
        return pl.pallas_call(
            functools.partial(kernel, **static) if static else kernel,
            out_shape=outs,
            in_specs=[spec[x.dtype == jnp.int32] for x in ins],
            out_specs=[spec[x.dtype == jnp.int32] for x in outs],
            scratch_shapes=list(scratch),
            compiler_params=pltpu.CompilerParams(vmem_limit_bytes=VMEM_LIMIT),
            name=name,
        )(*ins)

    chunk = pltpu.VMEM((rows, features), jnp.bfloat16)
    token = pltpu.VMEM((8, BLK), jnp.float32)
    partial, hid_t, own_rows = call(
        forward_kernel,
        "forward",
        [positions, gate, up, weights, in_hbm(cot_own)],
        [
            pltpu.VMEM((shard_count, rows, features), jnp.bfloat16),
            pltpu.VMEM((width, tokens), jnp.bfloat16),
            chunk,
        ],
        [
            pltpu.VMEM((tokens, width), jnp.bfloat16),
            pltpu.VMEM((list_len, tokens, BLK), jnp.float32),
            pltpu.VMEM((out_blocks, tokens, BLK), jnp.float32),
        ],
    )

    pairs = {True: neighbour_pairs(shard_count, 0), False: neighbour_pairs(shard_count, 1)}

    def exchange(value, even):
        return in_vmem(lax.ppermute(value, "tensor", pairs[even]))

    even_got = exchange(cot_own, True)
    odd_got = exchange(cot_own, False)
    gots = []
    kinds = []
    extra = []
    for step in range(1, shard_count):
        for got, even in ((even_got, True), (odd_got, False)):
            if brings_rows(shard_count, step, even):
                gots.append(got)
                kinds.append((step, even))
        if step == shard_count - 1:
            grads, send, cot, grads_done = call(
                block_grad_kernel,
                "block_grad",
                [positions, own_rows, *gots, hid_t],
                [
                    pltpu.VMEM((list_len * BLK, BLK), jnp.float32),
                    pltpu.VMEM((half, owned, BLK), jnp.bfloat16),
                    pltpu.VMEM((tokens, features), jnp.bfloat16),
                    token,
                ],
                shard_count=shard_count,
                kinds=tuple(kinds),
            )
            extra = [grads_done]
            from_core = in_vmem(lax.ppermute(send, "dp", [(s, s ^ 1) for s in range(replicas)]))
        (odd_send,) = call(relay_kernel, "relay_odd", [even_got, partial, *extra], [chunk], step=step + 1, even=False)
        (even_send,) = call(relay_kernel, "relay_even", [odd_got, partial, *extra], [chunk], step=step + 1, even=True)
        even_got, odd_got = exchange(even_send, True), exchange(odd_send, False)

    *pieces, own_sum, pairs_done = call(
        pair_kernel,
        "pair",
        [grads, from_core],
        [pltpu.VMEM((owned, BLK), jnp.bfloat16)] * (half - 1) + [pltpu.VMEM((owned, BLK), jnp.float32), token],
    )
    others = []
    for s in range(1, half):
        others.append(in_vmem(lax.ppermute(pieces[s - 1], "dp", [(e, e ^ (2 * s)) for e in range(replicas)])))

    gate_grad, up_grad, hidden_done = call(
        hidden_grad_kernel,
        "hidden_grad",
        [positions, cot, weights, gate, up, pairs_done],
        [jax.ShapeDtypeStruct((micro, shard_count, own, width), jnp.bfloat16)] * 2 + [token],
        [
            pltpu.VMEM((list_len, tokens, BLK), jnp.float32),
            pltpu.VMEM((width // BLK, tokens, BLK), jnp.float32),
        ],
    )
    (layer_out,) = call(
        layer_kernel,
        "layer",
        [even_got, odd_got, partial, hidden_done],
        [jax.ShapeDtypeStruct((rows, features), jnp.bfloat16)],
    )
    (block_grad,) = call(
        total_kernel,
        "total",
        [own_sum, *others],
        [jax.ShapeDtypeStruct((owned, BLK), jnp.float32)],
        replicas=replicas,
    )
    return (
        layer_out.reshape(micro, own, features),
        gate_grad.reshape(gate_pre.shape),
        up_grad.reshape(up_pre.shape),
        block_grad[None],
    )


def solution(mesh):
    return jax.shard_map(
        shards,
        mesh=mesh,
        in_specs=(
            P(None, "dp", "tensor"),
            P(None, "dp", "tensor"),
            P("tensor", None, None, None),
            P("tensor", None),
            P(None, ("dp", "tensor"), None),
        ),
        out_specs=(
            P(None, ("dp", "tensor"), None),
            P(None, "dp", "tensor"),
            P(None, "dp", "tensor"),
            P("tensor", "dp", None),
        ),
        check_vma=False,
    )
```

```python
import functools

import jax
import jax.numpy as jnp
from jax import lax
from jax.experimental import pallas as pl
from jax.experimental.pallas import tpu as pltpu
from jax.sharding import PartitionSpec as P


BLK = 128
VMEM_LIMIT = 24 << 20
LAST_STREAMS = 1
MID_STREAMS = {True: 2, False: 2}
HEAD = ("E0", "M0", "M1", "F")
MIDDLE = ("E0", "M0", "E1", "M1")
TAIL = ("grads", "core", "E0", "M0", "pair", "other", "hidden", "finish")
FIRST_STREAMS = {True: 1, False: 2}


def plan(shard_count, half):
    steps = []
    for word in HEAD:
        if word == "F":
            steps.append(("forward",))
        else:
            steps.append(("send", 1, word[0] == "E", int(word[1:])))
    for step in range(2, shard_count):
        for word in MIDDLE:
            key = (step, word[0] == "E", int(word[1:]))
            steps += [("relay", *key), ("send", *key)]
    for word in TAIL:
        if word[0] in "EM":
            key = (shard_count, word[0] == "E", int(word[1:]))
            steps += [("relay", *key), ("send", *key)]
        elif word == "other":
            steps += [("other", s) for s in range(1, half)]
        else:
            steps.append((word,))
    return steps


def in_vmem(value):
    return pltpu.with_memory_space_constraint(value, pltpu.VMEM)


def in_hbm(value):
    return pltpu.with_memory_space_constraint(value, pltpu.HBM)


def lanes(block):
    return pl.ds(pl.multiple_of(block * BLK, BLK), BLK)


def sources(place, step, even):
    parity_right = (place % 2 == 0) == even if isinstance(place, int) else (place % 2 == 0) if even else (place % 2 != 0)
    if isinstance(place, int):
        return place + step if parity_right else place - step
    return jnp.where(parity_right, place + step, place - step)


def brings_rows(shard_count, step, even):
    return any(0 <= sources(s, step, even) < shard_count for s in range(shard_count))


def forward_kernel(pos_ref, gate_ref, up_ref, w_ref, own_ref, p_ref, hid_t_ref, own_out_ref, gate_out_ref, up_out_ref, w_out_ref, hid_ref, prod_ref, acc_ref):
    micro, shard_count, own, width = gate_ref.shape
    gate_out_ref[...] = gate_ref[...]
    up_out_ref[...] = up_ref[...]
    w_out_ref[...] = w_ref[...]
    out_blocks = p_ref.shape[2] // BLK
    rows = micro * own
    own_out_ref[...] = own_ref[...]
    for j in range(shard_count):
        parts = []
        for m in range(micro):
            g = gate_ref[m, j].astype(jnp.float32)
            u = up_ref[m, j].astype(jnp.float32)
            parts.append(g * jax.nn.sigmoid(g) * u)
        hid_ref[pl.ds(j * rows, rows), :] = jnp.concatenate(parts, axis=0).astype(jnp.bfloat16)
    list_len = w_ref.shape[0]
    for n in range(list_len):
        c = pos_ref[n] // out_blocks
        prod_ref[n] = jnp.dot(hid_ref[:, lanes(c)], w_ref[n], preferred_element_type=jnp.float32)
    acc_ref[...] = jnp.zeros_like(acc_ref)
    for n in range(list_len):
        r = pos_ref[n] % out_blocks
        acc_ref[r] += prod_ref[n]
    for r in range(out_blocks):
        for j in range(shard_count):
            p_ref[j, :, pl.ds(r * BLK, BLK)] = acc_ref[r, pl.ds(j * rows, rows), :].astype(jnp.bfloat16)
    for c in range(width // BLK):
        hid_t_ref[pl.ds(c * BLK, BLK), :] = hid_ref[:, pl.ds(c * BLK, BLK)].T


def relay_kernel(*refs, step, even, stream):
    got_refs = refs[:-2]
    p_ref, send_ref = refs[-2:]
    shard_count = p_ref.shape[0]
    span = send_ref.shape[1]
    got_span = got_refs[0].shape[1]
    width = min(span, got_span)
    i = lax.axis_index("tensor")
    mirror = shard_count - 1 - i
    rightward = i % 2 == 0 if even else i % 2 != 0
    place = jnp.where(rightward, i, mirror)
    target = jnp.where(rightward, shard_count + 1 + i - step, step - 2 - mirror)
    adds = step >= place + 2
    first = place == 0
    for base in range(0, span, width):
        start = stream * span + base
        cols = pl.ds(base, width)
        p_cols = pl.ds(start, width)
        got_ref = got_refs[start // got_span if len(got_refs) > 1 else 0]
        got_cols = pl.ds(start % got_span, width)

        @pl.when(first)
        def _(cols=cols, p_cols=p_cols):
            send_ref[:, cols] = p_ref[target, :, p_cols]

        @pl.when(jnp.logical_and(adds, jnp.logical_not(first)))
        def _(cols=cols, p_cols=p_cols, got_ref=got_ref, got_cols=got_cols):
            both = got_ref[:, got_cols].astype(jnp.float32) + p_ref[target, :, p_cols].astype(jnp.float32)
            send_ref[:, cols] = both.astype(jnp.bfloat16)

        @pl.when(jnp.logical_not(adds))
        def _(cols=cols, got_ref=got_ref, got_cols=got_cols):
            send_ref[:, cols] = got_ref[:, got_cols]


def finish_kernel(*refs, streams, replicas):
    even_refs = refs[:streams]
    odd_refs = refs[streams:2 * streams]
    p_ref, sum_ref, *other_refs, out_ref, grad_ref = refs[2 * streams:]
    shard_count = p_ref.shape[0]
    i = lax.axis_index("tensor")
    even_alone = jnp.logical_and(i % 2 == 0, i == shard_count - 1)
    odd_alone = jnp.logical_or(i == 0, jnp.logical_and(i % 2 != 0, i == shard_count - 1))
    span = even_refs[0].shape[1]
    total = sum_ref[...]
    for other_ref in other_refs:
        total = total + other_ref[...].astype(jnp.float32)
    grad_ref[...] = total * (1.0 / replicas)
    for h in range(streams):
        cols = pl.ds(h * span, span)
        even_ref = even_refs[h]
        odd_ref = odd_refs[h]

        @pl.when(jnp.logical_not(jnp.logical_or(even_alone, odd_alone)))
        def _(even_ref=even_ref, odd_ref=odd_ref, cols=cols):
            both = even_ref[...].astype(jnp.float32) + odd_ref[...].astype(jnp.float32)
            out_ref[:, cols] = (p_ref[i, :, cols].astype(jnp.float32) + both).astype(jnp.bfloat16)

        @pl.when(odd_alone)
        def _(even_ref=even_ref, cols=cols):
            both = p_ref[i, :, cols].astype(jnp.float32) + even_ref[...].astype(jnp.float32)
            out_ref[:, cols] = both.astype(jnp.bfloat16)

        @pl.when(even_alone)
        def _(odd_ref=odd_ref, cols=cols):
            both = p_ref[i, :, cols].astype(jnp.float32) + odd_ref[...].astype(jnp.float32)
            out_ref[:, cols] = both.astype(jnp.bfloat16)


def block_grad_kernel(pos_ref, own_ref, *refs, shard_count, kinds):
    gots = refs[:len(kinds)]
    hid_t_ref, grad_ref, send_ref, cot_ref = refs[len(kinds):]
    rows, features = own_ref.shape
    out_blocks = features // BLK
    i = lax.axis_index("tensor")
    core = lax.axis_index("dp") % 2

    def rows_of(j):
        return pl.ds(pl.multiple_of(j * rows, rows), rows)

    cot_ref[rows_of(i), :] = own_ref[...]
    for got_ref, (step, even, stream) in zip(gots, kinds):
        source = sources(i, step, even)
        span = got_ref.shape[1]
        cols = pl.ds(stream * span, span)

        @pl.when(jnp.logical_and(source >= 0, source < shard_count))
        def _(got_ref=got_ref, source=source, cols=cols):
            cot_ref[rows_of(source), cols] = got_ref[...]

    for n in range(pos_ref.shape[0]):
        c = pos_ref[n] // out_blocks
        r = pos_ref[n] % out_blocks
        grad_ref[pl.ds(n * BLK, BLK), :] = jnp.dot(
            hid_t_ref[lanes(c), :], cot_ref[:, lanes(r)], preferred_element_type=jnp.float32
        )
    half, owned, _ = send_ref.shape
    for q in range(half):
        first = pl.multiple_of((2 * q + 1 - core) * owned, owned)
        send_ref[q] = grad_ref[pl.ds(first, owned), :].astype(jnp.bfloat16)


def pair_kernel(grad_ref, got_ref, *refs):
    own_ref = refs[-1]
    half, owned, _ = got_ref.shape
    d = lax.axis_index("dp")
    core = d % 2
    chip = d // 2

    def pair_sum(q):
        first = pl.multiple_of((2 * q + core) * owned, owned)
        return grad_ref[pl.ds(first, owned), :] + got_ref[q].astype(jnp.float32)

    for s in range(1, half):
        refs[s - 1][...] = pair_sum(jnp.bitwise_xor(chip, s)).astype(jnp.bfloat16)
    own_ref[...] = pair_sum(chip)


def hidden_grad_kernel(pos_ref, cot_ref, w_ref, gate_ref, up_ref, gg_ref, ug_ref, prod_ref, acc_ref):
    micro, shard_count, own, width = gate_ref.shape
    out_blocks = cot_ref.shape[1] // BLK
    rows = micro * own
    list_len = w_ref.shape[0]
    for n in range(list_len):
        r = pos_ref[n] % out_blocks
        prod_ref[n] = lax.dot_general(
            cot_ref[:, lanes(r)], w_ref[n], (((1,), (1,)), ((), ())), preferred_element_type=jnp.float32
        )
    acc_ref[...] = jnp.zeros_like(acc_ref)
    for n in range(list_len):
        c = pos_ref[n] // out_blocks
        acc_ref[c] += prod_ref[n]
    for c in range(width // BLK):
        cols = pl.ds(c * BLK, BLK)
        for j in range(shard_count):
            for m in range(micro):
                hg = acc_ref[c, pl.ds(j * rows + m * own, own), :]
                g = gate_ref[m, j, :, cols].astype(jnp.float32)
                u = up_ref[m, j, :, cols].astype(jnp.float32)
                s = jax.nn.sigmoid(g)
                gg_ref[m, j, :, cols] = (hg * u * s * (1.0 + g * (1.0 - s))).astype(jnp.bfloat16)
                ug_ref[m, j, :, cols] = (hg * (g * s)).astype(jnp.bfloat16)


def neighbour_pairs(replicas, size, first):
    table = list(range(size))
    for s in range(first, size - 1, 2):
        table[s], table[s + 1] = s + 1, s
    pairs = []
    for e in range(replicas):
        for s in range(size):
            partner = e * size + table[s] if table[s] != s else (e ^ 1) * size + s
            pairs.append((e * size + s, partner))
    return pairs


def shards(gate_pre, up_pre, down_blocks, block_index, out_grad):
    shard_count = lax.axis_size("tensor")
    replicas = lax.axis_size("dp")
    micro, token_rows, width = gate_pre.shape
    own = out_grad.shape[1]
    features = out_grad.shape[2]
    out_blocks = features // BLK
    rows = micro * own
    tokens = micro * token_rows
    list_len = block_index.shape[1]
    owned = list_len * BLK // replicas
    half = replicas // 2
    weights = in_hbm(down_blocks[0])
    gate = in_hbm(gate_pre.reshape(micro, shard_count, own, width))
    up = in_hbm(up_pre.reshape(micro, shard_count, own, width))
    cot_own = out_grad.reshape(rows, features)
    positions = in_hbm(block_index[0])
    vmem = pl.BlockSpec(memory_space=pltpu.VMEM)
    smem = pl.BlockSpec(memory_space=pltpu.SMEM)

    def call(kernel, ins, outs, scratch=(), **static):
        spec = {True: smem, False: vmem}
        return pl.pallas_call(
            functools.partial(kernel, **static) if static else kernel,
            out_shape=outs,
            in_specs=[spec[x.dtype == jnp.int32] for x in ins],
            out_specs=[vmem] * len(outs),
            scratch_shapes=list(scratch),
            compiler_params=pltpu.CompilerParams(vmem_limit_bytes=VMEM_LIMIT),
        )(*ins)

    pairs = {even: neighbour_pairs(replicas, shard_count, 0 if even else 1) for even in (True, False)}
    last = shard_count
    sends = {}
    got = {}
    values = {}

    def received(step, even, h, streams):
        mine = [got[key] for key in sorted(key for key in got if key[:2] == (step, even))]
        return [mine[h]] if len(mine) == streams else mine if streams == 1 or len(mine) == 1 else None

    def forward():
        values["partial"], values["hid_t"], values["own"], *values["inputs"] = call(
            forward_kernel,
            [positions, gate, up, weights, in_hbm(cot_own)],
            [
                pltpu.VMEM((shard_count, rows, features), jnp.bfloat16),
                pltpu.VMEM((width, tokens), jnp.bfloat16),
                pltpu.VMEM((rows, features), jnp.bfloat16),
                pltpu.VMEM(gate.shape, jnp.bfloat16),
                pltpu.VMEM(up.shape, jnp.bfloat16),
                pltpu.VMEM(weights.shape, jnp.bfloat16),
            ],
            [
                pltpu.VMEM((tokens, width), jnp.bfloat16),
                pltpu.VMEM((list_len, tokens, BLK), jnp.float32),
                pltpu.VMEM((out_blocks, tokens, BLK), jnp.float32),
            ],
        )

    def relay(step, even, h):
        streams = LAST_STREAMS if step == last else MID_STREAMS[even]
        (sends[step, even, h],) = call(
            relay_kernel,
            [*received(step - 1, not even, h, streams), values["partial"]],
            [pltpu.VMEM((rows, features // streams), jnp.bfloat16)],
            step=step,
            even=even,
            stream=h,
        )

    def send(step, even, h):
        if step == 1:
            streams = FIRST_STREAMS[even]
            wide = features // streams
            value = cot_own if streams == 1 else cot_own[:, h * wide:(h + 1) * wide]
        else:
            value = sends[step, even, h]
        got[step, even, h] = in_vmem(lax.ppermute(value, ("dp", "tensor"), pairs[even]))

    def grads():
        keys = [key for key in got if key[0] < last and brings_rows(shard_count, key[0], key[1])]
        values["grads"], values["for_core"], values["cot"] = call(
            block_grad_kernel,
            [positions, values["own"], *[got[key] for key in keys], values["hid_t"]],
            [
                pltpu.VMEM((list_len * BLK, BLK), jnp.float32),
                pltpu.VMEM((half, owned, BLK), jnp.bfloat16),
                pltpu.VMEM((tokens, features), jnp.bfloat16),
            ],
            shard_count=shard_count,
            kinds=tuple(keys),
        )

    def core():
        values["from_core"] = in_vmem(lax.ppermute(values["for_core"], "dp", [(s, s ^ 1) for s in range(replicas)]))

    def pair():
        *values["pieces"], values["sum"] = call(
            pair_kernel,
            [values["grads"], values["from_core"]],
            [pltpu.VMEM((owned, BLK), jnp.bfloat16)] * (half - 1) + [pltpu.VMEM((owned, BLK), jnp.float32)],
        )

    def other(s):
        value = lax.ppermute(values["pieces"][s - 1], "dp", [(e, e ^ (2 * s)) for e in range(replicas)])
        values["other", s] = in_vmem(value)

    def hidden():
        values["gate_grad"], values["up_grad"] = call(
            hidden_grad_kernel,
            [positions, values["cot"], values["inputs"][2], *values["inputs"][:2]],
            [jax.ShapeDtypeStruct((micro, shard_count, own, width), jnp.bfloat16)] * 2,
            [
                pltpu.VMEM((list_len, tokens, BLK), jnp.float32),
                pltpu.VMEM((width // BLK, tokens, BLK), jnp.float32),
            ],
        )

    def finish():
        gots = [got[last, even, h] for even in (True, False) for h in range(LAST_STREAMS)]
        values["layer_out"], values["block_grad"] = call(
            finish_kernel,
            [*gots, values["partial"], values["sum"], *[values["other", s] for s in range(1, half)]],
            [jax.ShapeDtypeStruct((rows, features), jnp.bfloat16), jax.ShapeDtypeStruct((owned, BLK), jnp.float32)],
            streams=LAST_STREAMS,
            replicas=replicas,
        )

    doers = dict(
        forward=forward, relay=relay, send=send, grads=grads, core=core, pair=pair, other=other, hidden=hidden, finish=finish
    )
    for action in plan(shard_count, half):
        doers[action[0]](*action[1:])
    layer_out, block_grad = values["layer_out"], values["block_grad"]
    gate_grad, up_grad = values["gate_grad"], values["up_grad"]
    return (
        layer_out.reshape(micro, own, features),
        gate_grad.reshape(gate_pre.shape),
        up_grad.reshape(up_pre.shape),
        block_grad[None],
    )


def solution(mesh):
    return jax.shard_map(
        shards,
        mesh=mesh,
        in_specs=(
            P(None, "dp", "tensor"),
            P(None, "dp", "tensor"),
            P("tensor", None, None, None),
            P("tensor", None),
            P(None, ("dp", "tensor"), None),
        ),
        out_specs=(
            P(None, ("dp", "tensor"), None),
            P(None, "dp", "tensor"),
            P(None, "dp", "tensor"),
            P("tensor", "dp", None),
        ),
        check_vma=False,
    )
```

```python
import functools

import jax
import jax.numpy as jnp
from jax import lax
from jax.experimental import pallas as pl
from jax.experimental.pallas import tpu as pltpu
from jax.sharding import PartitionSpec as P


BLK = 128
VMEM_LIMIT = 24 << 20
LAST_STREAMS = {True: 1, False: 1}
MID_STREAMS = {True: 2, False: 2}
HEAD = ("E0", "M0", "M1", "F")
MIDDLE = ("E0", "M0", "E1", "M1")
TAIL = ("gather", "grads", "core", "E0", "M0", "pair", "other", "hidden", "finish")
FIRST_STREAMS = {True: 1, False: 2}


def plan(shard_count, half):
    steps = []
    for word in HEAD:
        if word == "F":
            steps.append(("forward",))
        else:
            steps.append(("send", 1, word[0] == "E", int(word[1:])))
    for step in range(2, shard_count):
        for word in MIDDLE:
            key = (step, word[0] == "E", int(word[1:]))
            steps += [("relay", *key), ("send", *key)]
    for word in TAIL:
        if word[0] in "EM":
            key = (shard_count, word[0] == "E", int(word[1:]))
            steps += [("relay", *key), ("send", *key)]
        elif word == "other":
            steps += [("other", s) for s in range(half - 1, 0, -1)]
        else:
            steps.append((word,))
    return steps


def in_vmem(value):
    return pltpu.with_memory_space_constraint(value, pltpu.VMEM)


def in_hbm(value):
    return pltpu.with_memory_space_constraint(value, pltpu.HBM)


def lanes(block):
    return pl.ds(pl.multiple_of(block * BLK, BLK), BLK)


def sources(place, step, even):
    parity_right = (place % 2 == 0) == even if isinstance(place, int) else (place % 2 == 0) if even else (place % 2 != 0)
    if isinstance(place, int):
        return place + step if parity_right else place - step
    return jnp.where(parity_right, place + step, place - step)


def brings_rows(shard_count, step, even):
    return any(0 <= sources(s, step, even) < shard_count for s in range(shard_count))


def forward_kernel(pos_ref, gate_ref, up_ref, w_ref, own_ref, p_ref, hid_t_ref, own_out_ref, gate_out_ref, up_out_ref, w_out_ref, hid_ref, prod_ref, acc_ref):
    micro, shard_count, own, width = gate_ref.shape
    gate_out_ref[...] = gate_ref[...]
    up_out_ref[...] = up_ref[...]
    w_out_ref[...] = w_ref[...]
    out_blocks = p_ref.shape[2] // BLK
    rows = micro * own
    own_out_ref[...] = own_ref[...]
    for j in range(shard_count):
        parts = []
        for m in range(micro):
            g = gate_ref[m, j].astype(jnp.float32)
            u = up_ref[m, j].astype(jnp.float32)
            parts.append(g * jax.nn.sigmoid(g) * u)
        hid_ref[pl.ds(j * rows, rows), :] = jnp.concatenate(parts, axis=0).astype(jnp.bfloat16)
    list_len = w_ref.shape[0]
    for n in range(list_len):
        c = pos_ref[n] // out_blocks
        prod_ref[n] = jnp.dot(hid_ref[:, lanes(c)], w_ref[n], preferred_element_type=jnp.float32)
    acc_ref[...] = jnp.zeros_like(acc_ref)
    for n in range(list_len):
        r = pos_ref[n] % out_blocks
        acc_ref[r] += prod_ref[n]
    for r in range(out_blocks):
        for j in range(shard_count):
            p_ref[j, :, pl.ds(r * BLK, BLK)] = acc_ref[r, pl.ds(j * rows, rows), :].astype(jnp.bfloat16)
    for c in range(width // BLK):
        hid_t_ref[pl.ds(c * BLK, BLK), :] = hid_ref[:, pl.ds(c * BLK, BLK)].T


def relay_kernel(*refs, step, even, stream):
    got_refs = refs[:-2]
    p_ref, send_ref = refs[-2:]
    shard_count = p_ref.shape[0]
    span = send_ref.shape[1]
    got_span = got_refs[0].shape[1]
    width = min(span, got_span)
    i = lax.axis_index("tensor")
    mirror = shard_count - 1 - i
    rightward = i % 2 == 0 if even else i % 2 != 0
    place = jnp.where(rightward, i, mirror)
    target = jnp.where(rightward, shard_count + 1 + i - step, step - 2 - mirror)
    adds = step >= place + 2
    first = place == 0
    for base in range(0, span, width):
        start = stream * span + base
        cols = pl.ds(base, width)
        p_cols = pl.ds(start, width)
        got_ref = got_refs[start // got_span if len(got_refs) > 1 else 0]
        got_cols = pl.ds(start % got_span, width)

        @pl.when(first)
        def _(cols=cols, p_cols=p_cols):
            send_ref[:, cols] = p_ref[target, :, p_cols]

        @pl.when(jnp.logical_and(adds, jnp.logical_not(first)))
        def _(cols=cols, p_cols=p_cols, got_ref=got_ref, got_cols=got_cols):
            both = got_ref[:, got_cols].astype(jnp.float32) + p_ref[target, :, p_cols].astype(jnp.float32)
            send_ref[:, cols] = both.astype(jnp.bfloat16)

        @pl.when(jnp.logical_not(adds))
        def _(cols=cols, got_ref=got_ref, got_cols=got_cols):
            send_ref[:, cols] = got_ref[:, got_cols]


def finish_kernel(*refs, streams, replicas):
    even_refs = refs[:streams[0]]
    odd_refs = refs[streams[0]:sum(streams)]
    p_ref, sum_ref, *other_refs, out_ref, grad_ref = refs[sum(streams):]
    shard_count = p_ref.shape[0]
    i = lax.axis_index("tensor")
    even_alone = jnp.logical_and(i % 2 == 0, i == shard_count - 1)
    odd_alone = jnp.logical_or(i == 0, jnp.logical_and(i % 2 != 0, i == shard_count - 1))
    total = sum_ref[...]
    for other_ref in other_refs:
        total = total + other_ref[...].astype(jnp.float32)
    grad_ref[...] = total * (1.0 / replicas)
    span = out_ref.shape[1] // max(streams)

    def window(part_refs, start):
        width = part_refs[0].shape[1]
        return part_refs[start // width][:, pl.ds(start % width, span)].astype(jnp.float32)

    for start in range(0, out_ref.shape[1], span):
        cols = pl.ds(start, span)

        @pl.when(jnp.logical_not(jnp.logical_or(even_alone, odd_alone)))
        def _(start=start, cols=cols):
            both = window(even_refs, start) + window(odd_refs, start)
            out_ref[:, cols] = (p_ref[i, :, cols].astype(jnp.float32) + both).astype(jnp.bfloat16)

        @pl.when(odd_alone)
        def _(start=start, cols=cols):
            both = p_ref[i, :, cols].astype(jnp.float32) + window(even_refs, start)
            out_ref[:, cols] = both.astype(jnp.bfloat16)

        @pl.when(even_alone)
        def _(start=start, cols=cols):
            both = p_ref[i, :, cols].astype(jnp.float32) + window(odd_refs, start)
            out_ref[:, cols] = both.astype(jnp.bfloat16)


def place_rows(cot_ref, got_refs, kinds):
    rows = got_refs[0].shape[0]
    shard_count = cot_ref.shape[0] // rows
    i = lax.axis_index("tensor")
    for got_ref, (step, even, stream) in zip(got_refs, kinds):
        source = sources(i, step, even)
        span = got_ref.shape[1]
        cols = pl.ds(stream * span, span)

        @pl.when(jnp.logical_and(source >= 0, source < shard_count))
        def _(got_ref=got_ref, source=source, cols=cols):
            cot_ref[pl.ds(pl.multiple_of(source * rows, rows), rows), cols] = got_ref[...]


def gather_kernel(own_ref, *refs, kinds):
    *got_refs, cot_ref = refs
    rows = own_ref.shape[0]
    i = lax.axis_index("tensor")
    cot_ref[pl.ds(pl.multiple_of(i * rows, rows), rows), :] = own_ref[...]
    if got_refs:
        place_rows(cot_ref, got_refs, kinds)


def half_of_grads(pos_ref, hid_t_ref, cot_ref, out_ref, parity):
    half, owned, _ = out_ref.shape
    out_blocks = cot_ref.shape[1] // BLK
    piece = min(owned, BLK)
    for q in range(half):
        for part in range(owned // piece):
            start = (2 * q + parity) * owned + part * piece
            position = pos_ref[start // BLK]
            row = pl.multiple_of((position // out_blocks) * BLK + start % BLK, piece)
            grad = jnp.dot(
                hid_t_ref[pl.ds(row, piece), :],
                cot_ref[:, lanes(position % out_blocks)],
                preferred_element_type=jnp.float32,
            )
            out_ref[q, pl.ds(part * piece, piece), :] = grad.astype(out_ref.dtype)


def grads_kernel(pos_ref, cot_in_ref, hid_t_ref, *refs, kinds):
    *got_refs, cot_ref, send_ref, keep_ref = refs
    core = lax.axis_index("dp") % 2
    place_rows(cot_ref, got_refs, kinds)
    half_of_grads(pos_ref, hid_t_ref, cot_ref, send_ref, 1 - core)
    half_of_grads(pos_ref, hid_t_ref, cot_ref, keep_ref, core)


def pair_kernel(keep_ref, got_ref, *refs):
    half = got_ref.shape[0]
    chip = lax.axis_index("dp") // 2

    def pair_sum(q):
        return keep_ref[q] + got_ref[q].astype(jnp.float32)

    for s in range(1, half):
        refs[s - 1][...] = pair_sum(jnp.bitwise_xor(chip, s)).astype(jnp.bfloat16)
    refs[-1][...] = pair_sum(chip)


def hidden_grad_kernel(pos_ref, cot_ref, w_ref, gate_ref, up_ref, gg_ref, ug_ref, prod_ref, acc_ref):
    micro, shard_count, own, width = gate_ref.shape
    out_blocks = cot_ref.shape[1] // BLK
    rows = micro * own
    list_len = w_ref.shape[0]
    for n in range(list_len):
        r = pos_ref[n] % out_blocks
        prod_ref[n] = lax.dot_general(
            cot_ref[:, lanes(r)], w_ref[n], (((1,), (1,)), ((), ())), preferred_element_type=jnp.float32
        )
    acc_ref[...] = jnp.zeros_like(acc_ref)
    for n in range(list_len):
        c = pos_ref[n] // out_blocks
        acc_ref[c] += prod_ref[n]
    for c in range(width // BLK):
        cols = pl.ds(c * BLK, BLK)
        for j in range(shard_count):
            for m in range(micro):
                hg = acc_ref[c, pl.ds(j * rows + m * own, own), :]
                g = gate_ref[m, j, :, cols].astype(jnp.float32)
                u = up_ref[m, j, :, cols].astype(jnp.float32)
                s = jax.nn.sigmoid(g)
                gg_ref[m, j, :, cols] = (hg * u * s * (1.0 + g * (1.0 - s))).astype(jnp.bfloat16)
                ug_ref[m, j, :, cols] = (hg * (g * s)).astype(jnp.bfloat16)


def neighbour_pairs(replicas, size, first):
    table = list(range(size))
    for s in range(first, size - 1, 2):
        table[s], table[s + 1] = s + 1, s
    pairs = []
    for e in range(replicas):
        for s in range(size):
            partner = e * size + table[s] if table[s] != s else (e ^ 1) * size + s
            pairs.append((e * size + s, partner))
    return pairs


def shards(gate_pre, up_pre, down_blocks, block_index, out_grad):
    shard_count = lax.axis_size("tensor")
    replicas = lax.axis_size("dp")
    micro, token_rows, width = gate_pre.shape
    own = out_grad.shape[1]
    features = out_grad.shape[2]
    out_blocks = features // BLK
    rows = micro * own
    tokens = micro * token_rows
    list_len = block_index.shape[1]
    owned = list_len * BLK // replicas
    half = replicas // 2
    weights = in_hbm(down_blocks[0])
    gate = in_hbm(gate_pre.reshape(micro, shard_count, own, width))
    up = in_hbm(up_pre.reshape(micro, shard_count, own, width))
    cot_own = out_grad.reshape(rows, features)
    positions = in_hbm(block_index[0])
    vmem = pl.BlockSpec(memory_space=pltpu.VMEM)
    smem = pl.BlockSpec(memory_space=pltpu.SMEM)

    def call(kernel, ins, outs, scratch=(), aliases=None, **static):
        spec = {True: smem, False: vmem}
        return pl.pallas_call(
            functools.partial(kernel, **static) if static else kernel,
            out_shape=outs,
            in_specs=[spec[x.dtype == jnp.int32] for x in ins],
            out_specs=[vmem] * len(outs),
            scratch_shapes=list(scratch),
            input_output_aliases=aliases or {},
            compiler_params=pltpu.CompilerParams(vmem_limit_bytes=VMEM_LIMIT),
        )(*ins)

    pairs = {even: neighbour_pairs(replicas, shard_count, 0 if even else 1) for even in (True, False)}
    last = shard_count
    sends = {}
    got = {}
    values = {}

    def received(step, even, h, streams):
        mine = [got[key] for key in sorted(key for key in got if key[:2] == (step, even))]
        return [mine[h]] if len(mine) == streams else mine if streams == 1 or len(mine) == 1 else None

    def forward():
        values["partial"], values["hid_t"], values["own"], *values["inputs"] = call(
            forward_kernel,
            [positions, gate, up, weights, in_hbm(cot_own)],
            [
                pltpu.VMEM((shard_count, rows, features), jnp.bfloat16),
                pltpu.VMEM((width, tokens), jnp.bfloat16),
                pltpu.VMEM((rows, features), jnp.bfloat16),
                pltpu.VMEM(gate.shape, jnp.bfloat16),
                pltpu.VMEM(up.shape, jnp.bfloat16),
                pltpu.VMEM(weights.shape, jnp.bfloat16),
            ],
            [
                pltpu.VMEM((tokens, width), jnp.bfloat16),
                pltpu.VMEM((list_len, tokens, BLK), jnp.float32),
                pltpu.VMEM((out_blocks, tokens, BLK), jnp.float32),
            ],
        )

    def relay(step, even, h):
        streams = (LAST_STREAMS if step == last else MID_STREAMS)[even]
        (sends[step, even, h],) = call(
            relay_kernel,
            [*received(step - 1, not even, h, streams), values["partial"]],
            [pltpu.VMEM((rows, features // streams), jnp.bfloat16)],
            step=step,
            even=even,
            stream=h,
        )

    def send(step, even, h):
        if step == 1:
            streams = FIRST_STREAMS[even]
            wide = features // streams
            value = cot_own if streams == 1 else cot_own[:, h * wide:(h + 1) * wide]
        else:
            value = sends[step, even, h]
        got[step, even, h] = in_vmem(lax.ppermute(value, ("dp", "tensor"), pairs[even]))

    def arrivals(late):
        keys = [key for key in got if key[0] < last and brings_rows(shard_count, key[0], key[1])]
        return [key for key in keys if (key[0] == last - 1) == late]

    def gather():
        keys = arrivals(False)
        (values["gathered"],) = call(
            gather_kernel,
            [values["own"], *[got[key] for key in keys]],
            [pltpu.VMEM((tokens, features), jnp.bfloat16)],
            kinds=tuple(keys),
        )

    def grads():
        keys = arrivals(True)
        values["cot"], values["for_core"], values["keep"] = call(
            grads_kernel,
            [positions, in_vmem(values["gathered"]), values["hid_t"], *[got[key] for key in keys]],
            [
                pltpu.VMEM((tokens, features), jnp.bfloat16),
                pltpu.VMEM((half, owned, BLK), jnp.bfloat16),
                pltpu.VMEM((half, owned, BLK), jnp.float32),
            ],
            aliases={1: 0},
            kinds=tuple(keys),
        )

    def core():
        values["from_core"] = in_vmem(lax.ppermute(values["for_core"], "dp", [(s, s ^ 1) for s in range(replicas)]))

    def pair():
        *values["pieces"], values["sum"] = call(
            pair_kernel,
            [values["keep"], values["from_core"]],
            [pltpu.VMEM((owned, BLK), jnp.bfloat16)] * (half - 1) + [pltpu.VMEM((owned, BLK), jnp.float32)],
        )

    def other(s):
        value = lax.ppermute(values["pieces"][s - 1], "dp", [(e, e ^ (2 * s)) for e in range(replicas)])
        values["other", s] = in_vmem(value)

    def hidden():
        values["gate_grad"], values["up_grad"] = call(
            hidden_grad_kernel,
            [positions, values["cot"], values["inputs"][2], *values["inputs"][:2]],
            [jax.ShapeDtypeStruct((micro, shard_count, own, width), jnp.bfloat16)] * 2,
            [
                pltpu.VMEM((list_len, tokens, BLK), jnp.float32),
                pltpu.VMEM((width // BLK, tokens, BLK), jnp.float32),
            ],
        )

    def finish():
        gots = [got[last, even, h] for even in (True, False) for h in range(LAST_STREAMS[even])]
        values["layer_out"], values["block_grad"] = call(
            finish_kernel,
            [*gots, values["partial"], values["sum"], *[values["other", s] for s in range(1, half)]],
            [jax.ShapeDtypeStruct((rows, features), jnp.bfloat16), jax.ShapeDtypeStruct((owned, BLK), jnp.float32)],
            streams=(LAST_STREAMS[True], LAST_STREAMS[False]),
            replicas=replicas,
        )

    doers = dict(
        forward=forward, relay=relay, send=send, gather=gather, grads=grads, core=core, pair=pair, other=other, hidden=hidden, finish=finish
    )
    for action in plan(shard_count, half):
        doers[action[0]](*action[1:])
    layer_out, block_grad = values["layer_out"], values["block_grad"]
    gate_grad, up_grad = values["gate_grad"], values["up_grad"]
    return (
        layer_out.reshape(micro, own, features),
        gate_grad.reshape(gate_pre.shape),
        up_grad.reshape(up_pre.shape),
        block_grad[None],
    )


def solution(mesh):
    return jax.shard_map(
        shards,
        mesh=mesh,
        in_specs=(
            P(None, "dp", "tensor"),
            P(None, "dp", "tensor"),
            P("tensor", None, None, None),
            P("tensor", None),
            P(None, ("dp", "tensor"), None),
        ),
        out_specs=(
            P(None, ("dp", "tensor"), None),
            P(None, "dp", "tensor"),
            P(None, "dp", "tensor"),
            P("tensor", "dp", None),
        ),
        check_vma=False,
    )
```

```python
import functools

import jax
import jax.numpy as jnp
from jax import lax
from jax.experimental import pallas as pl
from jax.experimental.pallas import tpu as pltpu
from jax.sharding import PartitionSpec as P


BLK = 128
VMEM_LIMIT = 24 << 20
LAST_STREAMS = {True: 1, False: 1}
MID_STREAMS = {True: 2, False: 2}
HEAD = ("E0", "M0", "M1", "F")
MIDDLE = ("E0", "M0", "E1", "M1")
TAIL = ("gather", "grads", "core", "E0", "M0", "pair", "other", "hidden", "finish")
FIRST_STREAMS = {True: 1, False: 2}


def plan(shard_count, half):
    steps = []
    for word in HEAD:
        if word == "F":
            steps.append(("forward",))
        else:
            steps.append(("send", 1, word[0] == "E", int(word[1:])))
    for step in range(2, shard_count):
        for word in MIDDLE:
            key = (step, word[0] == "E", int(word[1:]))
            steps += [("relay", *key), ("send", *key)]
    for word in TAIL:
        if word[0] in "EM":
            key = (shard_count, word[0] == "E", int(word[1:]))
            steps += [("relay", *key), ("send", *key)]
        elif word == "other":
            steps += [("other", s) for s in range(half - 1, 0, -1)]
        else:
            steps.append((word,))
    return steps


def in_vmem(value):
    return pltpu.with_memory_space_constraint(value, pltpu.VMEM)


def in_smem(value):
    return pltpu.with_memory_space_constraint(value, pltpu.SMEM)


def in_hbm(value):
    return pltpu.with_memory_space_constraint(value, pltpu.HBM)


def lanes(block):
    return pl.ds(pl.multiple_of(block * BLK, BLK), BLK)


def sources(place, step, even):
    parity_right = (place % 2 == 0) == even if isinstance(place, int) else (place % 2 == 0) if even else (place % 2 != 0)
    if isinstance(place, int):
        return place + step if parity_right else place - step
    return jnp.where(parity_right, place + step, place - step)


def brings_rows(shard_count, step, even):
    return any(0 <= sources(s, step, even) < shard_count for s in range(shard_count))


def forward_kernel(pos_ref, gate_ref, up_ref, w_ref, own_ref, p_ref, hid_t_ref, own_out_ref, gate_out_ref, up_out_ref, w_out_ref, pos_out_ref, hid_ref, prod_ref, acc_ref):
    micro, shard_count, own, width = gate_ref.shape
    gate_out_ref[...] = gate_ref[...]
    up_out_ref[...] = up_ref[...]
    w_out_ref[...] = w_ref[...]
    out_blocks = p_ref.shape[2] // BLK
    rows = micro * own
    own_out_ref[...] = own_ref[...]
    for j in range(shard_count):
        parts = []
        for m in range(micro):
            g = gate_ref[m, j].astype(jnp.float32)
            u = up_ref[m, j].astype(jnp.float32)
            parts.append(g * jax.nn.sigmoid(g) * u)
        hid_ref[pl.ds(j * rows, rows), :] = jnp.concatenate(parts, axis=0).astype(jnp.bfloat16)
    list_len = w_ref.shape[0]
    for n in range(list_len):
        pos_out_ref[n] = pos_ref[n]
    for n in range(list_len):
        c = pos_ref[n] // out_blocks
        prod_ref[n] = jnp.dot(hid_ref[:, lanes(c)], w_ref[n], preferred_element_type=jnp.float32)
    acc_ref[...] = jnp.zeros_like(acc_ref)
    for n in range(list_len):
        r = pos_ref[n] % out_blocks
        acc_ref[r] += prod_ref[n]
    for r in range(out_blocks):
        for j in range(shard_count):
            p_ref[j, :, pl.ds(r * BLK, BLK)] = acc_ref[r, pl.ds(j * rows, rows), :].astype(jnp.bfloat16)
    for c in range(width // BLK):
        hid_t_ref[pl.ds(c * BLK, BLK), :] = hid_ref[:, pl.ds(c * BLK, BLK)].T


def relay_kernel(*refs, step, even, stream):
    got_refs = refs[:-2]
    p_ref, send_ref = refs[-2:]
    shard_count = p_ref.shape[0]
    span = send_ref.shape[1]
    got_span = got_refs[0].shape[1]
    width = min(span, got_span)
    i = lax.axis_index("tensor")
    mirror = shard_count - 1 - i
    rightward = i % 2 == 0 if even else i % 2 != 0
    place = jnp.where(rightward, i, mirror)
    target = jnp.where(rightward, shard_count + 1 + i - step, step - 2 - mirror)
    adds = step >= place + 2
    first = place == 0
    for base in range(0, span, width):
        start = stream * span + base
        cols = pl.ds(base, width)
        p_cols = pl.ds(start, width)
        got_ref = got_refs[start // got_span if len(got_refs) > 1 else 0]
        got_cols = pl.ds(start % got_span, width)

        @pl.when(first)
        def _(cols=cols, p_cols=p_cols):
            send_ref[:, cols] = p_ref[target, :, p_cols]

        @pl.when(jnp.logical_and(adds, jnp.logical_not(first)))
        def _(cols=cols, p_cols=p_cols, got_ref=got_ref, got_cols=got_cols):
            both = got_ref[:, got_cols].astype(jnp.float32) + p_ref[target, :, p_cols].astype(jnp.float32)
            send_ref[:, cols] = both.astype(jnp.bfloat16)

        @pl.when(jnp.logical_not(adds))
        def _(cols=cols, got_ref=got_ref, got_cols=got_cols):
            send_ref[:, cols] = got_ref[:, got_cols]


def finish_kernel(*refs, streams, replicas):
    even_refs = refs[:streams[0]]
    odd_refs = refs[streams[0]:sum(streams)]
    p_ref, sum_ref, *other_refs, out_ref, grad_ref = refs[sum(streams):]
    shard_count = p_ref.shape[0]
    i = lax.axis_index("tensor")
    even_alone = jnp.logical_and(i % 2 == 0, i == shard_count - 1)
    odd_alone = jnp.logical_or(i == 0, jnp.logical_and(i % 2 != 0, i == shard_count - 1))
    total = sum_ref[...]
    for other_ref in other_refs:
        total = total + other_ref[...].astype(jnp.float32)
    grad_ref[...] = total * (1.0 / replicas)
    span = out_ref.shape[1] // max(streams)

    def window(part_refs, start):
        width = part_refs[0].shape[1]
        return part_refs[start // width][:, pl.ds(start % width, span)].astype(jnp.float32)

    for start in range(0, out_ref.shape[1], span):
        cols = pl.ds(start, span)

        @pl.when(jnp.logical_not(jnp.logical_or(even_alone, odd_alone)))
        def _(start=start, cols=cols):
            both = window(even_refs, start) + window(odd_refs, start)
            out_ref[:, cols] = (p_ref[i, :, cols].astype(jnp.float32) + both).astype(jnp.bfloat16)

        @pl.when(odd_alone)
        def _(start=start, cols=cols):
            both = p_ref[i, :, cols].astype(jnp.float32) + window(even_refs, start)
            out_ref[:, cols] = both.astype(jnp.bfloat16)

        @pl.when(even_alone)
        def _(start=start, cols=cols):
            both = p_ref[i, :, cols].astype(jnp.float32) + window(odd_refs, start)
            out_ref[:, cols] = both.astype(jnp.bfloat16)


def place_rows(cot_ref, got_refs, kinds):
    rows = got_refs[0].shape[0]
    shard_count = cot_ref.shape[0] // rows
    i = lax.axis_index("tensor")
    for got_ref, (step, even, stream) in zip(got_refs, kinds):
        source = sources(i, step, even)
        span = got_ref.shape[1]
        cols = pl.ds(stream * span, span)

        @pl.when(jnp.logical_and(source >= 0, source < shard_count))
        def _(got_ref=got_ref, source=source, cols=cols):
            cot_ref[pl.ds(pl.multiple_of(source * rows, rows), rows), cols] = got_ref[...]


def gather_kernel(own_ref, *refs, kinds):
    *got_refs, cot_ref = refs
    rows = own_ref.shape[0]
    i = lax.axis_index("tensor")
    cot_ref[pl.ds(pl.multiple_of(i * rows, rows), rows), :] = own_ref[...]
    if got_refs:
        place_rows(cot_ref, got_refs, kinds)


def half_of_grads(pos_ref, hid_t_ref, cot_ref, out_ref, parity):
    half, owned, _ = out_ref.shape
    out_blocks = cot_ref.shape[1] // BLK
    piece = min(owned, BLK)
    for q in range(half):
        for part in range(owned // piece):
            start = (2 * q + parity) * owned + part * piece
            position = pos_ref[start // BLK]
            row = pl.multiple_of((position // out_blocks) * BLK + start % BLK, piece)
            grad = jnp.dot(
                hid_t_ref[pl.ds(row, piece), :],
                cot_ref[:, lanes(position % out_blocks)],
                preferred_element_type=jnp.float32,
            )
            out_ref[q, pl.ds(part * piece, piece), :] = grad.astype(out_ref.dtype)


def grads_kernel(pos_ref, cot_in_ref, hid_t_ref, *refs, kinds):
    *got_refs, cot_ref, send_ref, keep_ref = refs
    core = lax.axis_index("dp") % 2
    place_rows(cot_ref, got_refs, kinds)
    half_of_grads(pos_ref, hid_t_ref, cot_ref, send_ref, 1 - core)
    half_of_grads(pos_ref, hid_t_ref, cot_ref, keep_ref, core)


def pair_kernel(keep_ref, got_ref, *refs):
    half = got_ref.shape[0]
    chip = lax.axis_index("dp") // 2

    def pair_sum(q):
        return keep_ref[q] + got_ref[q].astype(jnp.float32)

    for s in range(1, half):
        refs[s - 1][...] = pair_sum(jnp.bitwise_xor(chip, s)).astype(jnp.bfloat16)
    refs[-1][...] = pair_sum(chip)


def hidden_grad_kernel(pos_ref, cot_ref, w_ref, gate_ref, up_ref, gg_ref, ug_ref, prod_ref, acc_ref):
    micro, shard_count, own, width = gate_ref.shape
    out_blocks = cot_ref.shape[1] // BLK
    rows = micro * own
    list_len = w_ref.shape[0]
    for n in range(list_len):
        r = pos_ref[n] % out_blocks
        prod_ref[n] = lax.dot_general(
            cot_ref[:, lanes(r)], w_ref[n], (((1,), (1,)), ((), ())), preferred_element_type=jnp.float32
        )
    acc_ref[...] = jnp.zeros_like(acc_ref)
    for n in range(list_len):
        c = pos_ref[n] // out_blocks
        acc_ref[c] += prod_ref[n]
    for c in range(width // BLK):
        cols = pl.ds(c * BLK, BLK)
        for j in range(shard_count):
            for m in range(micro):
                hg = acc_ref[c, pl.ds(j * rows + m * own, own), :]
                g = gate_ref[m, j, :, cols].astype(jnp.float32)
                u = up_ref[m, j, :, cols].astype(jnp.float32)
                s = jax.nn.sigmoid(g)
                gg_ref[m, j, :, cols] = (hg * u * s * (1.0 + g * (1.0 - s))).astype(jnp.bfloat16)
                ug_ref[m, j, :, cols] = (hg * (g * s)).astype(jnp.bfloat16)


def neighbour_pairs(replicas, size, first):
    table = list(range(size))
    for s in range(first, size - 1, 2):
        table[s], table[s + 1] = s + 1, s
    pairs = []
    for e in range(replicas):
        for s in range(size):
            partner = e * size + table[s] if table[s] != s else (e ^ 1) * size + s
            pairs.append((e * size + s, partner))
    return pairs


def shards(gate_pre, up_pre, down_blocks, block_index, out_grad):
    shard_count = lax.axis_size("tensor")
    replicas = lax.axis_size("dp")
    micro, token_rows, width = gate_pre.shape
    own = out_grad.shape[1]
    features = out_grad.shape[2]
    out_blocks = features // BLK
    rows = micro * own
    tokens = micro * token_rows
    list_len = block_index.shape[1]
    owned = list_len * BLK // replicas
    half = replicas // 2
    weights = in_hbm(down_blocks[0])
    gate = in_hbm(gate_pre.reshape(micro, shard_count, own, width))
    up = in_hbm(up_pre.reshape(micro, shard_count, own, width))
    cot_own = out_grad.reshape(rows, features)
    positions = in_hbm(block_index[0])
    vmem = pl.BlockSpec(memory_space=pltpu.VMEM)
    smem = pl.BlockSpec(memory_space=pltpu.SMEM)

    def call(kernel, ins, outs, scratch=(), aliases=None, **static):
        spec = {True: smem, False: vmem}
        return pl.pallas_call(
            functools.partial(kernel, **static) if static else kernel,
            out_shape=outs,
            in_specs=[spec[x.dtype == jnp.int32] for x in ins],
            out_specs=[spec[x.dtype == jnp.int32] for x in outs],
            scratch_shapes=list(scratch),
            input_output_aliases=aliases or {},
            compiler_params=pltpu.CompilerParams(vmem_limit_bytes=VMEM_LIMIT),
        )(*ins)

    pairs = {even: neighbour_pairs(replicas, shard_count, 0 if even else 1) for even in (True, False)}
    last = shard_count
    sends = {}
    got = {}
    values = {}

    def received(step, even, h, streams):
        mine = [got[key] for key in sorted(key for key in got if key[:2] == (step, even))]
        return [mine[h]] if len(mine) == streams else mine if streams == 1 or len(mine) == 1 else None

    def forward():
        values["partial"], values["hid_t"], values["own"], *values["inputs"] = call(
            forward_kernel,
            [positions, gate, up, weights, in_hbm(cot_own)],
            [
                pltpu.VMEM((shard_count, rows, features), jnp.bfloat16),
                pltpu.VMEM((width, tokens), jnp.bfloat16),
                pltpu.VMEM((rows, features), jnp.bfloat16),
                pltpu.VMEM(gate.shape, jnp.bfloat16),
                pltpu.VMEM(up.shape, jnp.bfloat16),
                pltpu.VMEM(weights.shape, jnp.bfloat16),
                pltpu.SMEM((list_len,), jnp.int32),
            ],
            [
                pltpu.VMEM((tokens, width), jnp.bfloat16),
                pltpu.VMEM((list_len, tokens, BLK), jnp.float32),
                pltpu.VMEM((out_blocks, tokens, BLK), jnp.float32),
            ],
        )

    def relay(step, even, h):
        streams = (LAST_STREAMS if step == last else MID_STREAMS)[even]
        (sends[step, even, h],) = call(
            relay_kernel,
            [*received(step - 1, not even, h, streams), values["partial"]],
            [pltpu.VMEM((rows, features // streams), jnp.bfloat16)],
            step=step,
            even=even,
            stream=h,
        )

    def send(step, even, h):
        if step == 1:
            streams = FIRST_STREAMS[even]
            wide = features // streams
            value = cot_own if streams == 1 else cot_own[:, h * wide:(h + 1) * wide]
        else:
            value = sends[step, even, h]
        got[step, even, h] = in_vmem(lax.ppermute(value, ("dp", "tensor"), pairs[even]))

    def arrivals(late):
        keys = [key for key in got if key[0] < last and brings_rows(shard_count, key[0], key[1])]
        return [key for key in keys if (key[0] == last - 1) == late]

    def gather():
        keys = arrivals(False)
        (values["gathered"],) = call(
            gather_kernel,
            [values["own"], *[got[key] for key in keys]],
            [pltpu.VMEM((tokens, features), jnp.bfloat16)],
            kinds=tuple(keys),
        )

    def grads():
        keys = arrivals(True)
        values["cot"], values["for_core"], values["keep"] = call(
            grads_kernel,
            [in_smem(values["inputs"][3]), in_vmem(values["gathered"]), values["hid_t"], *[got[key] for key in keys]],
            [
                pltpu.VMEM((tokens, features), jnp.bfloat16),
                pltpu.VMEM((half, owned, BLK), jnp.bfloat16),
                pltpu.VMEM((half, owned, BLK), jnp.float32),
            ],
            aliases={1: 0},
            kinds=tuple(keys),
        )

    def core():
        values["from_core"] = in_vmem(lax.ppermute(values["for_core"], "dp", [(s, s ^ 1) for s in range(replicas)]))

    def pair():
        *values["pieces"], values["sum"] = call(
            pair_kernel,
            [values["keep"], values["from_core"]],
            [pltpu.VMEM((owned, BLK), jnp.bfloat16)] * (half - 1) + [pltpu.VMEM((owned, BLK), jnp.float32)],
        )

    def other(s):
        value = lax.ppermute(values["pieces"][s - 1], "dp", [(e, e ^ (2 * s)) for e in range(replicas)])
        values["other", s] = in_vmem(value)

    def hidden():
        values["gate_grad"], values["up_grad"] = call(
            hidden_grad_kernel,
            [in_smem(values["inputs"][3]), values["cot"], values["inputs"][2], *values["inputs"][:2]],
            [jax.ShapeDtypeStruct((micro, shard_count, own, width), jnp.bfloat16)] * 2,
            [
                pltpu.VMEM((list_len, tokens, BLK), jnp.float32),
                pltpu.VMEM((width // BLK, tokens, BLK), jnp.float32),
            ],
        )

    def finish():
        gots = [got[last, even, h] for even in (True, False) for h in range(LAST_STREAMS[even])]
        values["layer_out"], values["block_grad"] = call(
            finish_kernel,
            [*gots, values["partial"], values["sum"], *[values["other", s] for s in range(1, half)]],
            [jax.ShapeDtypeStruct((rows, features), jnp.bfloat16), jax.ShapeDtypeStruct((owned, BLK), jnp.float32)],
            streams=(LAST_STREAMS[True], LAST_STREAMS[False]),
            replicas=replicas,
        )

    doers = dict(
        forward=forward, relay=relay, send=send, gather=gather, grads=grads, core=core, pair=pair, other=other, hidden=hidden, finish=finish
    )
    for action in plan(shard_count, half):
        doers[action[0]](*action[1:])
    layer_out, block_grad = values["layer_out"], values["block_grad"]
    gate_grad, up_grad = values["gate_grad"], values["up_grad"]
    return (
        layer_out.reshape(micro, own, features),
        gate_grad.reshape(gate_pre.shape),
        up_grad.reshape(up_pre.shape),
        block_grad[None],
    )


def solution(mesh):
    return jax.shard_map(
        shards,
        mesh=mesh,
        in_specs=(
            P(None, "dp", "tensor"),
            P(None, "dp", "tensor"),
            P("tensor", None, None, None),
            P("tensor", None),
            P(None, ("dp", "tensor"), None),
        ),
        out_specs=(
            P(None, ("dp", "tensor"), None),
            P(None, "dp", "tensor"),
            P(None, "dp", "tensor"),
            P("tensor", "dp", None),
        ),
        check_vma=False,
    )
```

```python
import functools

import jax
import jax.numpy as jnp
from jax import lax
from jax.experimental import pallas as pl
from jax.experimental.pallas import tpu as pltpu
from jax.sharding import PartitionSpec as P


BLK = 128
VMEM_LIMIT = 24 << 20
LAST_STREAMS = {True: 1, False: 1}
MID_STREAMS = {True: 2, False: 2}
HEAD = ("E0", "M0", "M1", "F")
MIDDLE = ("E0", "M0", "E1", "M1")
TAIL = ("gather", "grads", "core", "E0", "M0", "pair", "other", "hidden", "total", "finish")
FIRST_STREAMS = {True: 1, False: 2}


def plan(shard_count, half):
    steps = []
    for word in HEAD:
        if word == "F":
            steps.append(("forward",))
        else:
            steps.append(("send", 1, word[0] == "E", int(word[1:])))
    for step in range(2, shard_count):
        for word in MIDDLE:
            key = (step, word[0] == "E", int(word[1:]))
            steps += [("relay", *key), ("send", *key)]
    for word in TAIL:
        if word[0] in "EM":
            key = (shard_count, word[0] == "E", int(word[1:]))
            steps += [("relay", *key), ("send", *key)]
        elif word == "other":
            steps += [("other", s) for s in range(half - 1, 0, -1)]
        else:
            steps.append((word,))
    return steps


def in_vmem(value):
    return pltpu.with_memory_space_constraint(value, pltpu.VMEM)


def in_smem(value):
    return pltpu.with_memory_space_constraint(value, pltpu.SMEM)


def in_hbm(value):
    return pltpu.with_memory_space_constraint(value, pltpu.HBM)


def lanes(block):
    return pl.ds(pl.multiple_of(block * BLK, BLK), BLK)


def sources(place, step, even):
    parity_right = (place % 2 == 0) == even if isinstance(place, int) else (place % 2 == 0) if even else (place % 2 != 0)
    if isinstance(place, int):
        return place + step if parity_right else place - step
    return jnp.where(parity_right, place + step, place - step)


def brings_rows(shard_count, step, even):
    return any(0 <= sources(s, step, even) < shard_count for s in range(shard_count))


def forward_kernel(pos_ref, gate_ref, up_ref, w_ref, own_ref, p_ref, hid_t_ref, own_out_ref, gate_out_ref, up_out_ref, w_out_ref, pos_out_ref, hid_ref, prod_ref, acc_ref):
    micro, shard_count, own, width = gate_ref.shape
    gate_out_ref[...] = gate_ref[...]
    up_out_ref[...] = up_ref[...]
    w_out_ref[...] = w_ref[...]
    out_blocks = p_ref.shape[2] // BLK
    rows = micro * own
    own_out_ref[...] = own_ref[...]
    for j in range(shard_count):
        parts = []
        for m in range(micro):
            g = gate_ref[m, j].astype(jnp.float32)
            u = up_ref[m, j].astype(jnp.float32)
            parts.append(g * jax.nn.sigmoid(g) * u)
        hid_ref[pl.ds(j * rows, rows), :] = jnp.concatenate(parts, axis=0).astype(jnp.bfloat16)
    list_len = w_ref.shape[0]
    for n in range(list_len):
        pos_out_ref[n] = pos_ref[n]
    for n in range(list_len):
        c = pos_ref[n] // out_blocks
        prod_ref[n] = jnp.dot(hid_ref[:, lanes(c)], w_ref[n], preferred_element_type=jnp.float32)
    acc_ref[...] = jnp.zeros_like(acc_ref)
    for n in range(list_len):
        r = pos_ref[n] % out_blocks
        acc_ref[r] += prod_ref[n]
    for r in range(out_blocks):
        for j in range(shard_count):
            p_ref[j, :, pl.ds(r * BLK, BLK)] = acc_ref[r, pl.ds(j * rows, rows), :].astype(jnp.bfloat16)
    for c in range(width // BLK):
        hid_t_ref[pl.ds(c * BLK, BLK), :] = hid_ref[:, pl.ds(c * BLK, BLK)].T


def relay_kernel(*refs, step, even, stream):
    got_refs = refs[:-2]
    p_ref, send_ref = refs[-2:]
    shard_count = p_ref.shape[0]
    span = send_ref.shape[1]
    got_span = got_refs[0].shape[1]
    width = min(span, got_span)
    i = lax.axis_index("tensor")
    mirror = shard_count - 1 - i
    rightward = i % 2 == 0 if even else i % 2 != 0
    place = jnp.where(rightward, i, mirror)
    target = jnp.where(rightward, shard_count + 1 + i - step, step - 2 - mirror)
    adds = step >= place + 2
    first = place == 0
    for base in range(0, span, width):
        start = stream * span + base
        cols = pl.ds(base, width)
        p_cols = pl.ds(start, width)
        got_ref = got_refs[start // got_span if len(got_refs) > 1 else 0]
        got_cols = pl.ds(start % got_span, width)

        @pl.when(first)
        def _(cols=cols, p_cols=p_cols):
            send_ref[:, cols] = p_ref[target, :, p_cols]

        @pl.when(jnp.logical_and(adds, jnp.logical_not(first)))
        def _(cols=cols, p_cols=p_cols, got_ref=got_ref, got_cols=got_cols):
            both = got_ref[:, got_cols].astype(jnp.float32) + p_ref[target, :, p_cols].astype(jnp.float32)
            send_ref[:, cols] = both.astype(jnp.bfloat16)

        @pl.when(jnp.logical_not(adds))
        def _(cols=cols, got_ref=got_ref, got_cols=got_cols):
            send_ref[:, cols] = got_ref[:, got_cols]


def total_kernel(sum_ref, *refs, replicas):
    total = sum_ref[...]
    for other_ref in refs[:-1]:
        total = total + other_ref[...].astype(jnp.float32)
    refs[-1][...] = total * (1.0 / replicas)


def finish_kernel(*refs, streams):
    even_refs = refs[:streams[0]]
    odd_refs = refs[streams[0]:sum(streams)]
    p_ref, out_ref = refs[sum(streams):]
    shard_count = p_ref.shape[0]
    i = lax.axis_index("tensor")
    even_alone = jnp.logical_and(i % 2 == 0, i == shard_count - 1)
    odd_alone = jnp.logical_or(i == 0, jnp.logical_and(i % 2 != 0, i == shard_count - 1))
    span = out_ref.shape[1] // max(streams)

    def window(part_refs, start):
        width = part_refs[0].shape[1]
        return part_refs[start // width][:, pl.ds(start % width, span)].astype(jnp.float32)

    for start in range(0, out_ref.shape[1], span):
        cols = pl.ds(start, span)

        @pl.when(jnp.logical_not(jnp.logical_or(even_alone, odd_alone)))
        def _(start=start, cols=cols):
            both = window(even_refs, start) + window(odd_refs, start)
            out_ref[:, cols] = (p_ref[i, :, cols].astype(jnp.float32) + both).astype(jnp.bfloat16)

        @pl.when(odd_alone)
        def _(start=start, cols=cols):
            both = p_ref[i, :, cols].astype(jnp.float32) + window(even_refs, start)
            out_ref[:, cols] = both.astype(jnp.bfloat16)

        @pl.when(even_alone)
        def _(start=start, cols=cols):
            both = p_ref[i, :, cols].astype(jnp.float32) + window(odd_refs, start)
            out_ref[:, cols] = both.astype(jnp.bfloat16)


def place_rows(cot_ref, got_refs, kinds):
    rows = got_refs[0].shape[0]
    shard_count = cot_ref.shape[0] // rows
    i = lax.axis_index("tensor")
    for got_ref, (step, even, stream) in zip(got_refs, kinds):
        source = sources(i, step, even)
        span = got_ref.shape[1]
        cols = pl.ds(stream * span, span)

        @pl.when(jnp.logical_and(source >= 0, source < shard_count))
        def _(got_ref=got_ref, source=source, cols=cols):
            cot_ref[pl.ds(pl.multiple_of(source * rows, rows), rows), cols] = got_ref[...]


def gather_kernel(own_ref, *refs, kinds):
    *got_refs, cot_ref = refs
    rows = own_ref.shape[0]
    i = lax.axis_index("tensor")
    cot_ref[pl.ds(pl.multiple_of(i * rows, rows), rows), :] = own_ref[...]
    if got_refs:
        place_rows(cot_ref, got_refs, kinds)


def half_of_grads(pos_ref, hid_t_ref, cot_ref, out_ref, parity):
    half, owned, _ = out_ref.shape
    out_blocks = cot_ref.shape[1] // BLK
    piece = min(owned, BLK)
    for q in range(half):
        for part in range(owned // piece):
            start = (2 * q + parity) * owned + part * piece
            position = pos_ref[start // BLK]
            row = pl.multiple_of((position // out_blocks) * BLK + start % BLK, piece)
            grad = jnp.dot(
                hid_t_ref[pl.ds(row, piece), :],
                cot_ref[:, lanes(position % out_blocks)],
                preferred_element_type=jnp.float32,
            )
            out_ref[q, pl.ds(part * piece, piece), :] = grad.astype(out_ref.dtype)


def grads_kernel(pos_ref, cot_in_ref, hid_t_ref, *refs, kinds):
    *got_refs, cot_ref, send_ref, keep_ref = refs
    core = lax.axis_index("dp") % 2
    place_rows(cot_ref, got_refs, kinds)
    half_of_grads(pos_ref, hid_t_ref, cot_ref, send_ref, 1 - core)
    half_of_grads(pos_ref, hid_t_ref, cot_ref, keep_ref, core)


def pair_kernel(keep_ref, got_ref, *refs):
    half = got_ref.shape[0]
    chip = lax.axis_index("dp") // 2

    def pair_sum(q):
        return keep_ref[q] + got_ref[q].astype(jnp.float32)

    for s in range(1, half):
        refs[s - 1][...] = pair_sum(jnp.bitwise_xor(chip, s)).astype(jnp.bfloat16)
    refs[-1][...] = pair_sum(chip)


def hidden_grad_kernel(pos_ref, cot_ref, w_ref, gate_ref, up_ref, gg_ref, ug_ref, prod_ref, acc_ref):
    micro, shard_count, own, width = gate_ref.shape
    out_blocks = cot_ref.shape[1] // BLK
    rows = micro * own
    list_len = w_ref.shape[0]
    for n in range(list_len):
        r = pos_ref[n] % out_blocks
        prod_ref[n] = lax.dot_general(
            cot_ref[:, lanes(r)], w_ref[n], (((1,), (1,)), ((), ())), preferred_element_type=jnp.float32
        )
    acc_ref[...] = jnp.zeros_like(acc_ref)
    for n in range(list_len):
        c = pos_ref[n] // out_blocks
        acc_ref[c] += prod_ref[n]
    for c in range(width // BLK):
        cols = pl.ds(c * BLK, BLK)
        for j in range(shard_count):
            for m in range(micro):
                hg = acc_ref[c, pl.ds(j * rows + m * own, own), :]
                g = gate_ref[m, j, :, cols].astype(jnp.float32)
                u = up_ref[m, j, :, cols].astype(jnp.float32)
                s = jax.nn.sigmoid(g)
                gg_ref[m, j, :, cols] = (hg * u * s * (1.0 + g * (1.0 - s))).astype(jnp.bfloat16)
                ug_ref[m, j, :, cols] = (hg * (g * s)).astype(jnp.bfloat16)


def neighbour_pairs(replicas, size, first):
    table = list(range(size))
    for s in range(first, size - 1, 2):
        table[s], table[s + 1] = s + 1, s
    pairs = []
    for e in range(replicas):
        for s in range(size):
            partner = e * size + table[s] if table[s] != s else (e ^ 1) * size + s
            pairs.append((e * size + s, partner))
    return pairs


def shards(gate_pre, up_pre, down_blocks, block_index, out_grad):
    shard_count = lax.axis_size("tensor")
    replicas = lax.axis_size("dp")
    micro, token_rows, width = gate_pre.shape
    own = out_grad.shape[1]
    features = out_grad.shape[2]
    out_blocks = features // BLK
    rows = micro * own
    tokens = micro * token_rows
    list_len = block_index.shape[1]
    owned = list_len * BLK // replicas
    half = replicas // 2
    weights = in_hbm(down_blocks[0])
    gate = in_hbm(gate_pre.reshape(micro, shard_count, own, width))
    up = in_hbm(up_pre.reshape(micro, shard_count, own, width))
    cot_own = out_grad.reshape(rows, features)
    positions = in_hbm(block_index[0])
    vmem = pl.BlockSpec(memory_space=pltpu.VMEM)
    smem = pl.BlockSpec(memory_space=pltpu.SMEM)

    def call(kernel, ins, outs, scratch=(), aliases=None, **static):
        spec = {True: smem, False: vmem}
        return pl.pallas_call(
            functools.partial(kernel, **static) if static else kernel,
            out_shape=outs,
            in_specs=[spec[x.dtype == jnp.int32] for x in ins],
            out_specs=[spec[x.dtype == jnp.int32] for x in outs],
            scratch_shapes=list(scratch),
            input_output_aliases=aliases or {},
            compiler_params=pltpu.CompilerParams(vmem_limit_bytes=VMEM_LIMIT),
        )(*ins)

    pairs = {even: neighbour_pairs(replicas, shard_count, 0 if even else 1) for even in (True, False)}
    last = shard_count
    sends = {}
    got = {}
    values = {}

    def received(step, even, h, streams):
        mine = [got[key] for key in sorted(key for key in got if key[:2] == (step, even))]
        return [mine[h]] if len(mine) == streams else mine if streams == 1 or len(mine) == 1 else None

    def forward():
        values["partial"], values["hid_t"], values["own"], *values["inputs"] = call(
            forward_kernel,
            [positions, gate, up, weights, in_hbm(cot_own)],
            [
                pltpu.VMEM((shard_count, rows, features), jnp.bfloat16),
                pltpu.VMEM((width, tokens), jnp.bfloat16),
                pltpu.VMEM((rows, features), jnp.bfloat16),
                pltpu.VMEM(gate.shape, jnp.bfloat16),
                pltpu.VMEM(up.shape, jnp.bfloat16),
                pltpu.VMEM(weights.shape, jnp.bfloat16),
                pltpu.SMEM((list_len,), jnp.int32),
            ],
            [
                pltpu.VMEM((tokens, width), jnp.bfloat16),
                pltpu.VMEM((list_len, tokens, BLK), jnp.float32),
                pltpu.VMEM((out_blocks, tokens, BLK), jnp.float32),
            ],
        )

    def relay(step, even, h):
        streams = (LAST_STREAMS if step == last else MID_STREAMS)[even]
        (sends[step, even, h],) = call(
            relay_kernel,
            [*received(step - 1, not even, h, streams), values["partial"]],
            [pltpu.VMEM((rows, features // streams), jnp.bfloat16)],
            step=step,
            even=even,
            stream=h,
        )

    def send(step, even, h):
        if step == 1:
            streams = FIRST_STREAMS[even]
            wide = features // streams
            value = cot_own if streams == 1 else cot_own[:, h * wide:(h + 1) * wide]
        else:
            value = sends[step, even, h]
        got[step, even, h] = in_vmem(lax.ppermute(value, ("dp", "tensor"), pairs[even]))

    def arrivals(late):
        keys = [key for key in got if key[0] < last and brings_rows(shard_count, key[0], key[1])]
        return [key for key in keys if (key[0] == last - 1) == late]

    def gather():
        keys = arrivals(False)
        (values["gathered"],) = call(
            gather_kernel,
            [values["own"], *[got[key] for key in keys]],
            [pltpu.VMEM((tokens, features), jnp.bfloat16)],
            kinds=tuple(keys),
        )

    def grads():
        keys = arrivals(True)
        values["cot"], values["for_core"], values["keep"] = call(
            grads_kernel,
            [in_smem(values["inputs"][3]), in_vmem(values["gathered"]), values["hid_t"], *[got[key] for key in keys]],
            [
                pltpu.VMEM((tokens, features), jnp.bfloat16),
                pltpu.VMEM((half, owned, BLK), jnp.bfloat16),
                pltpu.VMEM((half, owned, BLK), jnp.float32),
            ],
            aliases={1: 0},
            kinds=tuple(keys),
        )

    def core():
        values["from_core"] = in_vmem(lax.ppermute(values["for_core"], "dp", [(s, s ^ 1) for s in range(replicas)]))

    def pair():
        *values["pieces"], values["sum"] = call(
            pair_kernel,
            [values["keep"], values["from_core"]],
            [pltpu.VMEM((owned, BLK), jnp.bfloat16)] * (half - 1) + [pltpu.VMEM((owned, BLK), jnp.float32)],
        )

    def other(s):
        value = lax.ppermute(values["pieces"][s - 1], "dp", [(e, e ^ (2 * s)) for e in range(replicas)])
        values["other", s] = in_vmem(value)

    def hidden():
        values["gate_grad"], values["up_grad"] = call(
            hidden_grad_kernel,
            [in_smem(values["inputs"][3]), values["cot"], values["inputs"][2], *values["inputs"][:2]],
            [jax.ShapeDtypeStruct((micro, shard_count, own, width), jnp.bfloat16)] * 2,
            [
                pltpu.VMEM((list_len, tokens, BLK), jnp.float32),
                pltpu.VMEM((width // BLK, tokens, BLK), jnp.float32),
            ],
        )

    def finish():
        gots = [got[last, even, h] for even in (True, False) for h in range(LAST_STREAMS[even])]
        (values["layer_out"],) = call(
            finish_kernel,
            [*gots, values["partial"]],
            [jax.ShapeDtypeStruct((rows, features), jnp.bfloat16)],
            streams=(LAST_STREAMS[True], LAST_STREAMS[False]),
        )

    def total():
        (values["block_grad"],) = call(
            total_kernel,
            [values["sum"], *[values["other", s] for s in range(1, half)]],
            [jax.ShapeDtypeStruct((owned, BLK), jnp.float32)],
            replicas=replicas,
        )

    doers = dict(
        forward=forward, relay=relay, send=send, gather=gather, grads=grads, core=core, pair=pair, other=other, hidden=hidden, finish=finish, total=total
    )
    for action in plan(shard_count, half):
        doers[action[0]](*action[1:])
    layer_out, block_grad = values["layer_out"], values["block_grad"]
    gate_grad, up_grad = values["gate_grad"], values["up_grad"]
    return (
        layer_out.reshape(micro, own, features),
        gate_grad.reshape(gate_pre.shape),
        up_grad.reshape(up_pre.shape),
        block_grad[None],
    )


def solution(mesh):
    return jax.shard_map(
        shards,
        mesh=mesh,
        in_specs=(
            P(None, "dp", "tensor"),
            P(None, "dp", "tensor"),
            P("tensor", None, None, None),
            P("tensor", None),
            P(None, ("dp", "tensor"), None),
        ),
        out_specs=(
            P(None, ("dp", "tensor"), None),
            P(None, "dp", "tensor"),
            P(None, "dp", "tensor"),
            P("tensor", "dp", None),
        ),
        check_vma=False,
    )
```
